256 devices in a mesh: seq: 16 (over y_lo, z), dp: 16 (over x, y_hi, core).
Axes of the slice: x: 4, y: 4 (y_hi: 2, y_lo: 2; y = y_hi * 2 + y_lo), z: 8, core: 2. Of those that a mesh axis runs over, the one named last changes fastest.
Arguments:
- layer_rows: bfloat16 [16, 2048, 1024], P('dp', 'seq'), may hold values from -6 to 6
- doc_ids: int32 [16, 2048], P('dp', 'seq'), may hold values from 0 to 5, never falling along the last dimension, each value on 1 to 1024 neighbouring positions
- packing: int32 [16, 16], P('dp'), may hold values from 0 to 15, each once within a row
- norm_gain: float32 [1024], replicated, may hold values from 0.1 to 1.9
- w_qkv: bfloat16 [1024, 3072], replicated, may hold values from -0.1875 to 0.1875
- d_attn: bfloat16 [16, 2048, 1024], P('dp', 'seq'), may hold values from -6 to 6
Outputs:
- d_input: bfloat16 [16, 2048, 1024], P('dp', 'seq')
- w_grad: float32 [1024, 3072], P('seq')
The draws below stay inside these ranges and needn't reach their ends.
Inputs may be any that keep to these rules, and one draw needn't show every extreme that they name: `doc_ids`: in each group the song numbers never fall along the initial order; every number occurs, and one song spans exactly 1024 frames. `packing`: each group's row names every block number once.
All inputs are finite; a program needn't handle non-finite values.
Results may differ from the reference program's by a relative error of at most 0.024.
Values may be sent and summed in bfloat16 or wider, within the bound.
No kernel may reach another device: no remote copies, remote signals or barrier semaphores. Data moves between devices by JAX's collectives and lax.ppermute only.
A program may use at most 128 MiB of HBM per device.

```python
import math
import jax
import jax.numpy as jnp
import numpy as np
from jax import lax

D = 1024
HEADS = 8
HEAD = 128
TOK_DEV = 128
BLOCK = 128
DOCS = 6
HD = 1024
SEQ_LEN = 2048
GROUPS = 16
NBLK = 16
ALL_TOKENS = 32768
N_SEQ = 16


def steps_of(own_key, extent, cuts, least, high):
    def one(position, blocks):
        heights = jax.random.uniform(jax.random.fold_in(jax.random.fold_in(own_key, 6), position), (blocks,), jnp.float32, least / len(cuts), high / len(cuts))
        return jnp.repeat(jnp.exp(heights), extent[position] // blocks).reshape((-1,) + (1,) * (len(extent) - position - 1))

    loudness = one(*cuts[0])
    for cut in cuts[1:]:
        loudness = loudness * one(*cut)
    return loudness


def profile(number_of, total, reach, skew):
    weights = [(1 << 20) // math.isqrt(rank ** skew) + 1 for rank in range(2, number_of + 1)]
    surplus, counts = total - reach - (number_of - 1), [1] * (number_of - 1)
    while surplus > 0:
        free = [i for i in range(number_of - 1) if counts[i] < reach]
        whole, left = sum([weights[i] for i in free]), surplus
        for i in free:
            extra = min(reach - counts[i], max(1, left * weights[i] // whole), surplus)
            counts[i] = counts[i] + extra
            surplus = surplus - extra
    return np.array([reach] + counts)


def uneven(key, count, total, reach, lean):
    if count == 2:
        one = jax.random.randint(key, (), max(1, total - reach), min(reach, total - 1) + 1)
        return jnp.stack([one, total - one])
    lengths = jnp.asarray(profile(count, total, reach, lean), jnp.int32)
    pairs = (count - 1) // 2
    source_of, receiver = lengths[1:1 + 2 * pairs:2], lengths[2:2 + 2 * pairs:2]
    margin = jnp.minimum(source_of - 1, reach - receiver)
    moved = jax.random.randint(jax.random.fold_in(key, 1), (pairs,), 0, 1 << 20) % (margin + 1)
    lengths = lengths.at[1:1 + 2 * pairs:2].set(source_of - moved).at[2:2 + 2 * pairs:2].set(receiver + moved)
    return lengths[jax.random.permutation(jax.random.fold_in(key, 2), count)]


def centred(stream_key, extent, scale, bound, shards=(), kind=jnp.bfloat16):
    loudness = steps_of(stream_key, extent, shards, -0.22, 0.18) if shards else 1.0
    drawn = jax.random.normal(stream_key, extent, jnp.float32) * scale * loudness
    return jnp.minimum(jnp.maximum(drawn, -bound), bound).astype(kind)


def setup_inputs(seed: int = 0) -> dict:
    keys = jax.random.split(jax.random.key(seed), 7)
    return {
        "layer_rows": centred(keys[0], (GROUPS, SEQ_LEN, D), 1.0, 6.0, ((0, 16), (1, 16))),
        "doc_ids": jax.vmap(lambda own: jnp.searchsorted(jnp.cumsum(uneven(own, DOCS, SEQ_LEN, SEQ_LEN // 2, 2)), jnp.arange(SEQ_LEN), side="right"))(jax.random.split(keys[1], GROUPS)).reshape((GROUPS, SEQ_LEN)).astype(jnp.int32),
        "packing": jax.vmap(lambda own: jax.random.permutation(own, NBLK))(jax.random.split(keys[2], GROUPS)).reshape((GROUPS, NBLK)).astype(jnp.int32),
        "norm_gain": jnp.clip(1.0 + 0.18 * jax.random.normal(keys[3], (D,), jnp.float32), 0.1, 1.9),
        "w_qkv": centred(keys[4], (D, 3 * HD), D ** -0.5, 0.1875),
        "d_attn": centred(keys[5], (GROUPS, SEQ_LEN, HD), 1.0, 6.0, ((0, 16), (1, 16))),
    }


def rounded(value):
    return lax.optimization_barrier(value.astype(jnp.bfloat16)).astype(jnp.float32)

def normalize(frames, norm_gain):
    values = frames.astype(jnp.float32)
    inverse = lax.rsqrt(lax.optimization_barrier(jnp.mean(values * values, axis=-1, keepdims=True)) + 1e-05)
    unit_rows = values * inverse
    return (inverse, unit_rows, (unit_rows * norm_gain).astype(jnp.bfloat16))

def shard_grads(queries, grad_out, query_docs, query_pos, all_keys, all_values, key_docs, key_pos):
    head_cols = HEADS * HEAD
    factor = 1.0 / math.sqrt(HEAD)
    q_heads = queries.astype(jnp.float32).reshape(-1, HEADS, HEAD)
    k_heads = all_keys.astype(jnp.float32).reshape(-1, HEADS, HEAD)
    v_heads = all_values.astype(jnp.float32).reshape(-1, HEADS, HEAD)
    g_heads = grad_out.astype(jnp.float32).reshape(-1, HEADS, HEAD)
    allowed = (query_docs[:, None] == key_docs[None, :]) & (key_pos[None, :] <= query_pos[:, None])
    scores = jnp.einsum('qhd,khd->hqk', q_heads, k_heads) * factor
    expon = jnp.where(allowed[None], jnp.exp(scores), jnp.float32(0.0))
    attn_prob = expon / lax.optimization_barrier(jnp.sum(expon, axis=-1, keepdims=True))
    prob_low = rounded(attn_prob)
    outputs = jnp.einsum('hqk,khd->qhd', prob_low, v_heads)
    row_delta = lax.optimization_barrier(jnp.sum(g_heads * outputs, axis=-1))
    grad_prob = jnp.einsum('qhd,khd->hqk', g_heads, v_heads)
    dscore = rounded(attn_prob * (grad_prob - row_delta.T[:, :, None]))
    dquery = jnp.einsum('hqk,khd->qhd', dscore, k_heads) * factor
    dkey = jnp.einsum('hqk,qhd->khd', dscore, q_heads) * factor
    dvalue = jnp.einsum('hqk,qhd->khd', prob_low, g_heads)
    key_part = jnp.concatenate([dkey.reshape(-1, head_cols), dvalue.reshape(-1, head_cols)], axis=1)
    return (dquery.reshape(-1, head_cols), rounded(key_part))

def reference(layer_rows, doc_ids, packing, norm_gain, w_qkv, d_attn):
    head_cols = HEADS * HEAD
    shard_ids = jnp.arange(N_SEQ, dtype=jnp.int32)

    def group_grads(w_sum, inputs):
        rows_group, doc_group, pack_group, grad_group = inputs
        packed = rows_group.reshape(NBLK, BLOCK, D)[pack_group].reshape(SEQ_LEN, D)
        packed_docs = doc_group.reshape(NBLK, BLOCK)[pack_group].reshape(SEQ_LEN)
        positions = (pack_group[:, None] * BLOCK + jnp.arange(BLOCK, dtype=jnp.int32)[None, :]).reshape(SEQ_LEN)
        inverse, unit_rows, normed = normalize(packed, norm_gain)
        projected = jnp.dot(normed, w_qkv, preferred_element_type=jnp.float32).astype(jnp.bfloat16)
        queries = projected[:, :head_cols]
        all_keys = projected[:, head_cols:2 * head_cols]
        all_values = projected[:, 2 * head_cols:]

        def per_shard(key_sum, shard_idx):
            first_row = (shard_idx * TOK_DEV).astype(jnp.int32)
            dquery, key_part = shard_grads(lax.dynamic_slice_in_dim(queries, first_row, TOK_DEV, 0), lax.dynamic_slice_in_dim(grad_group, first_row, TOK_DEV, 0), lax.dynamic_slice_in_dim(packed_docs, first_row, TOK_DEV, 0), lax.dynamic_slice_in_dim(positions, first_row, TOK_DEV, 0), all_keys, all_values, packed_docs, positions)
            return (key_sum + key_part, dquery)
        key_sum, dquery = lax.scan(per_shard, jnp.zeros((SEQ_LEN, 2 * head_cols), jnp.float32), shard_ids)
        grad_qkv = jnp.concatenate([dquery.reshape(SEQ_LEN, head_cols), key_sum], axis=1).astype(jnp.bfloat16)
        d_normed = jnp.dot(grad_qkv, w_qkv.T, preferred_element_type=jnp.float32)
        gained = d_normed * norm_gain
        d_frames = (inverse * (gained - unit_rows * lax.optimization_barrier(jnp.mean(gained * unit_rows, axis=-1, keepdims=True)))).astype(jnp.bfloat16)

        def weight_part(total, shard_idx):
            first_row = (shard_idx * TOK_DEV).astype(jnp.int32)
            normed_run = lax.dynamic_slice_in_dim(normed, first_row, TOK_DEV, 0)
            grads_run = lax.dynamic_slice_in_dim(grad_qkv, first_row, TOK_DEV, 0)
            return (total + rounded(jnp.dot(normed_run.T, grads_run, preferred_element_type=jnp.float32)), jnp.float32(0.0))
        w_sum, ignored = lax.scan(weight_part, w_sum, shard_ids)
        return (w_sum, d_frames)
    w_sum, d_input = lax.scan(group_grads, jnp.zeros((D, 3 * head_cols), jnp.float32), (layer_rows, doc_ids, packing, d_attn))
    w_grad = w_sum * (1.0 / math.sqrt(ALL_TOKENS))
    return (d_input, w_grad)
```

```python
import math

import jax
import jax.numpy as jnp
from jax import lax
from jax.experimental import pallas as pl
from jax.experimental.pallas import tpu as pltpu
from jax.sharding import Mesh
from jax.sharding import PartitionSpec as P

HEADS = 8
HEAD = 128
BLOCK = 128
HALF = 64
NBLK = 16
D = 1024
STEPS = 4
QROWS = 256
KROWS = 512
EXTRA = 8
FACTOR = 1.0 / math.sqrt(HEAD)
EPS = 1e-05
F32 = jnp.float32
BF16 = jnp.bfloat16


def dot(a, b, ca, cb):
    return lax.dot_general(a, b, (((ca,), (cb,)), ((), ())), preferred_element_type=F32)


def place_of(p):
    return (p % 8) * 2 + p // 8


def head_kernel(
    meta, pay, do, gain, wq, wk, wv,
    snd, dwk, dws,
    normed, q_s, do_s, k_s, v_s, dk_s, dv_s, dw_s, e_s, p_s, docs, inv,
):
    step = pl.program_id(0)
    half = meta[NBLK + 1]

    @pl.when(step == 0)
    def _():
        def put(p, carry):
            inv[meta[p]] = p
            return carry

        lax.fori_loop(0, NBLK, put, 0)
        docs[...] = jnp.full(docs.shape, 1000.0, F32)
        dk_s[...] = jnp.zeros(dk_s.shape, F32)
        dv_s[...] = jnp.zeros(dv_s.shape, F32)

    rows = pay[:, 0, 0:BLOCK, :].astype(F32)
    inverse = lax.rsqrt(jnp.mean(rows * rows, axis=-1, keepdims=True) + EPS)
    nrm = (rows * inverse * gain[...][None]).astype(BF16)
    normed[pl.ds(step * 4, 4)] = nrm
    nrm = nrm.reshape(KROWS, D)
    k_s[step] = dot(nrm, wk[...], 1, 0).astype(BF16)
    v_s[step] = dot(nrm, wv[...], 1, 0).astype(BF16)
    own = pl.multiple_of(half * HALF, HALF)
    qn = normed[pl.ds(step * 4, 4), pl.ds(own, HALF), :].reshape(QROWS, D)
    q_s[...] = dot(qn, wq[...], 1, 0).astype(BF16)
    for t in range(4):
        do_s[t * HALF : (t + 1) * HALF, :] = do[place_of(inv[step * 4 + t])]

    info = jnp.sum(pay[:, 0, BLOCK : BLOCK + EXTRA, 0:QROWS].astype(F32), axis=0)
    docs[step] = info
    mine = jnp.where(half == 0, info[0:1, :], info[1:2, :])
    lane = lax.broadcasted_iota(jnp.int32, (1, QROWS), 1)
    q_pos = step * KROWS + (lane // HALF) * BLOCK + half * HALF + lane % HALF
    known = docs[...]
    real = lax.broadcasted_iota(jnp.int32, known.shape, 1) < 2
    first = jnp.zeros((1, QROWS), F32)
    for number in range(1, 6):
        below = jnp.sum(jnp.where((known < number) & real, 1.0, 0.0))
        first = first + jnp.where(mine == number, below, 0.0)
    q_first = first.astype(jnp.int32)

    def scores(g, total):
        s = dot(k_s[g], q_s[...], 1, 1) * FACTOR
        j = g * KROWS + lax.broadcasted_iota(jnp.int32, (KROWS, QROWS), 0)
        e = jnp.where((j >= q_first) & (j <= q_pos), jnp.exp(s), 0.0)
        e_s[g] = e
        return total + jnp.sum(e, axis=0, keepdims=True)

    total = lax.fori_loop(0, step + 1, scores, jnp.zeros((1, QROWS), F32))
    scale = 1.0 / total

    def deltas(g, delta):
        grad = dot(v_s[g], do_s[...], 1, 1)
        p_s[g] = grad
        low = (e_s[g] * scale).astype(BF16)
        dv_s[g] += dot(low, do_s[...], 1, 0)
        return delta + jnp.sum(low.astype(F32) * grad, axis=0, keepdims=True)

    delta = lax.fori_loop(0, step + 1, deltas, jnp.zeros((1, QROWS), F32))

    def grads(g, dq):
        ds = (e_s[g] * scale * (p_s[g] - delta)).astype(BF16)
        dk_s[g] += dot(ds, q_s[...], 1, 0)
        return dq + dot(ds, k_s[g], 0, 0)

    dq = lax.fori_loop(0, step + 1, grads, jnp.zeros((QROWS, HEAD), F32))
    dq = (dq * FACTOR).astype(BF16)
    for t in range(4):
        snd[place_of(inv[step * 4 + t]), 0:HALF, :] = dq[t * HALF : (t + 1) * HALF, :]
    part = dot(dq, qn, 0, 0)

    @pl.when(step == 0)
    def _():
        dw_s[0:HEAD, :] = part

    @pl.when(step > 0)
    def _():
        dw_s[0:HEAD, :] += part

    @pl.when(step == STEPS - 1)
    def _():
        every = normed[...].reshape(NBLK * BLOCK, D)
        for n, grad in ((0, dk_s[...] * FACTOR), (1, dv_s[...])):
            grad = grad.astype(BF16).reshape(NBLK, BLOCK, HEAD)
            for b in range(NBLK):
                at = HALF + n * BLOCK
                snd[place_of(inv[b]), at : at + BLOCK, :] = grad[b]
            lo = HEAD * (n + 1)
            dw_s[lo : lo + HEAD, :] = dot(grad.reshape(NBLK * BLOCK, HEAD), every, 0, 0)
        y = meta[NBLK + 2]
        for u in range(2):
            for g in range(3):
                lo = u * 512
                turned = dw_s[g * HEAD : (g + 1) * HEAD, lo : lo + 512].T.astype(BF16)
                turned = turned.reshape(8, 2, 32, HEAD)
                to = jnp.where(y == u, 0, 1)
                even = turned[:, 0]
                odd = turned[:, 1]
                kept = jnp.where(half == 0, even, odd)
                sent = jnp.where(half == 0, odd, even)
                dwk[to, :, :, g * HEAD : (g + 1) * HEAD] = kept
                dws[to, :, :, g * HEAD : (g + 1) * HEAD] = sent


def head_pass(meta, payload, do, gain, w_qkv):
    grid_spec = pltpu.PrefetchScalarGridSpec(
        num_scalar_prefetch=1,
        grid=(STEPS,),
        in_specs=[
            pl.BlockSpec((4, 1, BLOCK + EXTRA, D), lambda i, m: (i % 2, i // 2, 0, 0)),
            pl.BlockSpec((NBLK, HALF, HEAD), lambda i, m: (0, 0, 0)),
            pl.BlockSpec((1, D), lambda i, m: (0, 0)),
            pl.BlockSpec((D, HEAD), lambda i, m: (0, m[NBLK])),
            pl.BlockSpec((D, HEAD), lambda i, m: (0, HEADS + m[NBLK])),
            pl.BlockSpec((D, HEAD), lambda i, m: (0, 2 * HEADS + m[NBLK])),
        ],
        out_specs=[
            pl.BlockSpec((NBLK, HALF + 2 * BLOCK, HEAD), lambda i, m: (0, 0, 0)),
            pl.BlockSpec((2, 8, 32, 3 * HEAD), lambda i, m: (0, 0, 0, 0)),
            pl.BlockSpec((2, 8, 32, 3 * HEAD), lambda i, m: (0, 0, 0, 0)),
        ],
        scratch_shapes=[
            pltpu.VMEM((NBLK, BLOCK, D), BF16),
            pltpu.VMEM((QROWS, HEAD), BF16),
            pltpu.VMEM((QROWS, HEAD), BF16),
            pltpu.VMEM((STEPS, KROWS, HEAD), BF16),
            pltpu.VMEM((STEPS, KROWS, HEAD), BF16),
            pltpu.VMEM((STEPS, KROWS, HEAD), F32),
            pltpu.VMEM((STEPS, KROWS, HEAD), F32),
            pltpu.VMEM((3 * HEAD, D), F32),
            pltpu.VMEM((STEPS, KROWS, QROWS), F32),
            pltpu.VMEM((STEPS, KROWS, QROWS), F32),
            pltpu.VMEM((STEPS, EXTRA, QROWS), F32),
            pltpu.SMEM((NBLK,), jnp.int32),
        ],
    )
    return pl.pallas_call(
        head_kernel,
        grid_spec=grid_spec,
        out_shape=[
            jax.ShapeDtypeStruct((NBLK, HALF + 2 * BLOCK, HEAD), BF16),
            jax.ShapeDtypeStruct((2, 8, 32, 3 * HEAD), BF16),
            jax.ShapeDtypeStruct((2, 8, 32, 3 * HEAD), BF16),
        ],
        name="head_pass",
    )(meta, payload, do, gain, w_qkv, w_qkv, w_qkv)


def rows_kernel(meta, back, pay, gain, w, out, grad, d_norm):
    step = pl.program_id(0)

    @pl.when(step == 0)
    def _():
        for h in range(HEADS):
            for c in range(2):
                grad[c * HALF : (c + 1) * HALF, h * HEAD : (h + 1) * HEAD] = back[h, c, 0:HALF, :]
            for n in range(2):
                lo = HALF + n * BLOCK
                both = back[h, 0, lo : lo + BLOCK, :].astype(F32) + back[h, 1, lo : lo + BLOCK, :].astype(F32)
                to = (n + 1) * D + h * HEAD
                grad[:, to : to + HEAD] = both.astype(BF16)

    d_norm[step] = dot(grad[...], w[...], 1, 1)

    @pl.when(step == STEPS - 1)
    def _():
        values = pay[0, 0, 0:BLOCK, :].astype(F32)
        inverse = lax.rsqrt(jnp.mean(values * values, axis=-1, keepdims=True) + EPS)
        unit = values * inverse
        gained = jnp.concatenate([d_norm[n] for n in range(STEPS)], axis=1) * gain[...]
        shared = jnp.mean(gained * unit, axis=-1, keepdims=True)
        out[...] = (inverse * (gained - unit * shared)).astype(BF16)


def rows_pass(meta, back, payload, gain, w_qkv):
    def block_of(i, m):
        b = m[m[NBLK + 1] * 8 + m[NBLK]]
        return (b % 8, b // 8, 0, 0)

    grid_spec = pltpu.PrefetchScalarGridSpec(
        num_scalar_prefetch=1,
        grid=(STEPS,),
        in_specs=[
            pl.BlockSpec((HEADS, 2, HALF + 2 * BLOCK, HEAD), lambda i, m: (0, 0, 0, 0)),
            pl.BlockSpec((1, 1, BLOCK + EXTRA, D), block_of),
            pl.BlockSpec((1, D), lambda i, m: (0, 0)),
            pl.BlockSpec((D // STEPS, 3 * D), lambda i, m: (i, 0)),
        ],
        out_specs=pl.BlockSpec((BLOCK, D), lambda i, m: (0, 0)),
        scratch_shapes=[
            pltpu.VMEM((BLOCK, 3 * D), BF16),
            pltpu.VMEM((STEPS, BLOCK, D // STEPS), F32),
        ],
    )
    return pl.pallas_call(
        rows_kernel,
        grid_spec=grid_spec,
        out_shape=jax.ShapeDtypeStruct((BLOCK, D), BF16),
        name="rows_pass",
    )(meta, back, payload, gain, w_qkv)


def flip(x, axis, bit, size):
    return lax.ppermute(x, axis, [(i, i ^ bit) for i in range(size)])


def turn(x):
    return lax.ppermute(x, ("y_lo", "core"), [(0, 0), (1, 2), (2, 1), (3, 3)])


def added(a, b):
    return (a.astype(F32) + b.astype(F32)).astype(BF16)


def body(layer_rows, doc_ids, packing, norm_gain, w_qkv, d_attn):
    z = lax.axis_index("z")
    y = lax.axis_index("y_lo")
    core = lax.axis_index("core")
    halves = doc_ids[0].astype(BF16).reshape(2, 1, HALF)
    at = (jnp.arange(4, dtype=jnp.int32) == z % 4).astype(BF16)[None, :, None]
    info = jnp.pad((halves * at).reshape(2, QROWS), ((0, EXTRA - 2), (0, D - QROWS)))
    payload = turn(jnp.concatenate([layer_rows[0], info], axis=0))
    order = turn(packing[0])
    pieces = d_attn[0].reshape(2, HALF, HEADS, HEAD).transpose(2, 0, 1, 3)
    pieces = turn(pieces.reshape(NBLK, HALF, HEAD))
    meta = jnp.concatenate([order, jnp.stack([z, core, y, y]).astype(jnp.int32)])
    gain = norm_gain[None, :]

    everything = lax.all_gather(payload, ("z", "core"), axis=0, tiled=False)
    everything = everything.reshape(8, 2, BLOCK + EXTRA, D)
    do = lax.all_to_all(pieces, ("z", "core"), 0, 0, tiled=True)
    snd, dwk, dws = head_pass(meta, everything, do, gain, w_qkv)

    w_sum = added(dwk, flip(dws, "core", 1, 2))
    w_sum = added(w_sum[0], flip(w_sum[1], "y_lo", 1, 2))
    back = lax.all_to_all(snd, ("z", "core"), 0, 0, tiled=True)
    w_sum = lax.all_to_all(w_sum, "z", 0, 0, tiled=True)
    back = back.reshape(HEADS, 2, HALF + 2 * BLOCK, HEAD)
    d_rows = turn(rows_pass(meta, back, everything, gain, w_qkv))

    w_sum = added(w_sum, flip(w_sum, "x", 1, 4))
    w_sum = added(w_sum, flip(w_sum, "x", 2, 4))
    w_sum = added(w_sum, flip(w_sum, "y_hi", 1, 2))
    other = flip(w_sum, "core", 1, 2)
    both = jnp.where(core == 0, jnp.stack([w_sum, other]), jnp.stack([other, w_sum]))
    both = both.reshape(2, HEADS, 32, 3, HEAD).transpose(0, 2, 3, 1, 4)
    w_grad = both.reshape(64, 3 * D).astype(F32) * (1.0 / math.sqrt(32768))
    return (d_rows[None], w_grad)


def solution(mesh):
    fine = Mesh(
        mesh.devices.reshape(2, 8, 4, 2, 2), ("y_lo", "z", "x", "y_hi", "core")
    )
    seq = ("y_lo", "z")
    dp = ("x", "y_hi", "core")
    return jax.shard_map(
        body,
        mesh=fine,
        in_specs=(
            P(dp, seq, None),
            P(dp, seq),
            P(dp, None),
            P(),
            P(),
            P(dp, seq, None),
        ),
        out_specs=(P(dp, seq, None), P(seq, None)),
        check_vma=False,
    )
```

```python
import math

import jax
import jax.numpy as jnp
from jax import lax
from jax.experimental import pallas as pl
from jax.experimental.pallas import tpu as pltpu
from jax.sharding import Mesh
from jax.sharding import PartitionSpec as P

HEADS = 8
HEAD = 128
BLOCK = 128
HALF = 64
NBLK = 16
D = 1024
STEPS = 4
QROWS = 256
KROWS = 512
EXTRA = 8
FACTOR = 1.0 / math.sqrt(HEAD)
EPS = 1e-05
F32 = jnp.float32
BF16 = jnp.bfloat16


def dot(a, b, ca, cb):
    return lax.dot_general(a, b, (((ca,), (cb,)), ((), ())), preferred_element_type=F32)


def place_of(p):
    return (p % 8) * 2 + p // 8


PIECES = 9


def head_kernel(*refs):
    meta, pieces, others, rest = refs[0], refs[1 : 1 + PIECES], refs[1 + PIECES : 1 + 2 * PIECES], refs[1 + 2 * PIECES :]
    (
        do, gain, wq, wk, wv,
        normed, mine, keep, send, dq_o, dk_o, dv_o,
        rows_s, q_s, do_s, k_s, v_s, dk_s, dv_s, e_s, p_s, docs, inv, sems,
    ) = rest
    step = pl.program_id(0)
    z = meta[NBLK]
    half = meta[NBLK + 1]

    @pl.when(step == 0)
    def _():
        copies = []
        for c, group in enumerate((pieces, others)):
            side = half if c == 0 else 1 - half
            for n, ref in enumerate(group):
                offset = (0, 1, 7, 2, 6, 3, 5, 4, 4)[n]
                target = rows_s.at[side * 8 + (z + offset) % 8]
                if n == 7:
                    target = target.at[0:HALF]
                elif n == 8:
                    target = target.at[HALF : BLOCK + EXTRA]
                copies.append(pltpu.make_async_copy(ref, target, sems.at[c * PIECES + n]))
        for copy in copies:
            copy.start()

        def put(p, carry):
            inv[meta[p]] = p
            return carry

        lax.fori_loop(0, NBLK, put, 0)
        docs[...] = jnp.full(docs.shape, 1000.0, F32)
        dk_s[...] = jnp.zeros(dk_s.shape, F32)
        dv_s[...] = jnp.zeros(dv_s.shape, F32)
        for copy in copies:
            copy.wait()
        mine[...] = rows_s[meta[half * 8 + z], 0:BLOCK, :]

    rows = rows_s[pl.ds(step * 4, 4), 0:BLOCK, :].astype(F32)
    inverse = lax.rsqrt(jnp.mean(rows * rows, axis=-1, keepdims=True) + EPS)
    nrm = (rows * inverse * gain[...][None]).astype(BF16)
    normed[...] = nrm
    nrm = nrm.reshape(KROWS, D)
    k_s[step] = dot(nrm, wk[...], 1, 0).astype(BF16)
    v_s[step] = dot(nrm, wv[...], 1, 0).astype(BF16)
    own = pl.multiple_of(half * HALF, HALF)
    qn = normed[:, pl.ds(own, HALF), :].reshape(QROWS, D)
    q_s[...] = dot(qn, wq[...], 1, 0).astype(BF16)
    for t in range(4):
        do_s[t * HALF : (t + 1) * HALF, :] = do[place_of(inv[step * 4 + t])]

    info = jnp.sum(rows_s[pl.ds(step * 4, 4), BLOCK : BLOCK + EXTRA, 0:QROWS].astype(F32), axis=0)
    docs[step] = info
    mine_docs = jnp.where(half == 0, info[0:1, :], info[1:2, :])
    lane = lax.broadcasted_iota(jnp.int32, (1, QROWS), 1)
    q_pos = step * KROWS + (lane // HALF) * BLOCK + half * HALF + lane % HALF
    known = docs[...]
    real = lax.broadcasted_iota(jnp.int32, known.shape, 1) < 2
    first = jnp.zeros((1, QROWS), F32)
    for number in range(1, 6):
        below = jnp.sum(jnp.where((known < number) & real, 1.0, 0.0))
        first = first + jnp.where(mine_docs == number, below, 0.0)
    q_first = first.astype(jnp.int32)

    def scores(g, total):
        s = dot(k_s[g], q_s[...], 1, 1) * FACTOR
        j = g * KROWS + lax.broadcasted_iota(jnp.int32, (KROWS, QROWS), 0)
        e = jnp.where((j >= q_first) & (j <= q_pos), jnp.exp(s), 0.0)
        e_s[g] = e
        return total + jnp.sum(e, axis=0, keepdims=True)

    total = lax.fori_loop(0, step + 1, scores, jnp.zeros((1, QROWS), F32))
    scale = 1.0 / total

    def deltas(g, delta):
        grad = dot(v_s[g], do_s[...], 1, 1)
        p_s[g] = grad
        low = (e_s[g] * scale).astype(BF16)
        dv_s[g] += dot(low, do_s[...], 1, 0)
        return delta + jnp.sum(low.astype(F32) * grad, axis=0, keepdims=True)

    delta = lax.fori_loop(0, step + 1, deltas, jnp.zeros((1, QROWS), F32))

    def grads(g, dq):
        ds = (e_s[g] * scale * (p_s[g] - delta)).astype(BF16)
        dk_s[g] += dot(ds, q_s[...], 1, 0)
        return dq + dot(ds, k_s[g], 0, 0)

    def place(b, lo, value):
        p = inv[b]
        same = p // 8 == half

        @pl.when(same)
        def _():
            keep[p % 8, lo : lo + value.shape[0], :] = value

        @pl.when(jnp.logical_not(same))
        def _():
            send[p % 8, lo : lo + value.shape[0], :] = value

    dq = lax.fori_loop(0, step + 1, grads, jnp.zeros((QROWS, HEAD), F32))
    dq = (dq * FACTOR).astype(BF16)
    dq_o[step] = dq
    for t in range(4):
        place(step * 4 + t, 0, dq[t * HALF : (t + 1) * HALF, :])

    @pl.when(step == STEPS - 1)
    def _():
        for n, grad, out in ((0, dk_s[...] * FACTOR, dk_o), (1, dv_s[...], dv_o)):
            grad = grad.astype(BF16)
            out[...] = grad
            grad = grad.reshape(NBLK, BLOCK, HEAD)
            for b in range(NBLK):
                place(b, HALF + n * BLOCK, grad[b])


def head_pass(meta, pieces, others, do, gain, w_qkv):
    whole = [(STEPS, QROWS, HEAD), (STEPS, KROWS, HEAD), (STEPS, KROWS, HEAD)]
    pack = (8, HALF + 2 * BLOCK, HEAD)
    grid_spec = pltpu.PrefetchScalarGridSpec(
        num_scalar_prefetch=1,
        grid=(STEPS,),
        in_specs=[pl.BlockSpec(memory_space=pl.ANY)] * (2 * PIECES)
        + [
            pl.BlockSpec((NBLK, HALF, HEAD), lambda i, m: (0, 0, 0)),
            pl.BlockSpec((1, D), lambda i, m: (0, 0)),
            pl.BlockSpec((D, HEAD), lambda i, m: (0, m[NBLK])),
            pl.BlockSpec((D, HEAD), lambda i, m: (0, HEADS + m[NBLK])),
            pl.BlockSpec((D, HEAD), lambda i, m: (0, 2 * HEADS + m[NBLK])),
        ],
        out_specs=[
            pl.BlockSpec((4, BLOCK, D), lambda i, m: (i, 0, 0)),
            pl.BlockSpec((BLOCK, D), lambda i, m: (0, 0)),
            pl.BlockSpec(pack, lambda i, m: (0, 0, 0)),
            pl.BlockSpec(pack, lambda i, m: (0, 0, 0)),
        ]
        + [pl.BlockSpec(shape, lambda i, m: (0, 0, 0)) for shape in whole],
        scratch_shapes=[
            pltpu.VMEM((NBLK, BLOCK + EXTRA, D), BF16),
            pltpu.VMEM((QROWS, HEAD), BF16),
            pltpu.VMEM((QROWS, HEAD), BF16),
            pltpu.VMEM((STEPS, KROWS, HEAD), BF16),
            pltpu.VMEM((STEPS, KROWS, HEAD), BF16),
            pltpu.VMEM((STEPS, KROWS, HEAD), F32),
            pltpu.VMEM((STEPS, KROWS, HEAD), F32),
            pltpu.VMEM((STEPS, KROWS, QROWS), F32),
            pltpu.VMEM((STEPS, KROWS, QROWS), F32),
            pltpu.VMEM((STEPS, EXTRA, QROWS), F32),
            pltpu.SMEM((NBLK,), jnp.int32),
            pltpu.SemaphoreType.DMA((2 * PIECES,)),
        ],
    )
    return pl.pallas_call(
        head_kernel,
        grid_spec=grid_spec,
        out_shape=[
            jax.ShapeDtypeStruct((NBLK, BLOCK, D), BF16),
            jax.ShapeDtypeStruct((BLOCK, D), BF16),
            jax.ShapeDtypeStruct(pack, BF16),
            jax.ShapeDtypeStruct(pack, BF16),
        ]
        + [jax.ShapeDtypeStruct(shape, BF16) for shape in whole],
        name="head_pass",
    )(meta, *pieces, *others, do, gain, w_qkv, w_qkv, w_qkv)


def weight_kernel(meta, normed, dq, dk, dv, dwk, dws, dw_s):
    step = pl.program_id(0)
    half = meta[NBLK + 1]
    y = meta[NBLK + 2]
    every = normed[...].reshape(KROWS, D)
    qn = normed[:, pl.ds(pl.multiple_of(half * HALF, HALF), HALF), :].reshape(QROWS, D)
    both = jnp.concatenate([dk[0], dv[0]], axis=1)
    parts = ((0, HEAD, dot(dq[0], qn, 0, 0)), (HEAD, 3 * HEAD, dot(both, every, 0, 0)))

    @pl.when(step == 0)
    def _():
        for lo, hi, part in parts:
            dw_s[lo:hi, :] = part

    @pl.when(step > 0)
    def _():
        for lo, hi, part in parts:
            dw_s[lo:hi, :] += part

    @pl.when(step == STEPS - 1)
    def _():
        for u in range(2):
            for g in range(3):
                turned = dw_s[g * HEAD : (g + 1) * HEAD, u * 512 : (u + 1) * 512].T
                turned = turned.reshape(8, 2, 4, 8, HEAD)
                to = jnp.where(y == u, 0, 1)
                for x in range(4):
                    even = turned[:, 0, x]
                    odd = turned[:, 1, x]
                    dwk[to, x, :, :, g * HEAD : (g + 1) * HEAD] = jnp.where(half == 0, even, odd).astype(BF16)
                    dws[to, x, :, :, g * HEAD : (g + 1) * HEAD] = jnp.where(half == 0, odd, even).astype(BF16)


def weight_pass(meta, normed, dq, dk, dv):
    shape = (2, 4, 8, 8, 3 * HEAD)
    grid_spec = pltpu.PrefetchScalarGridSpec(
        num_scalar_prefetch=1,
        grid=(STEPS,),
        in_specs=[
            pl.BlockSpec((4, BLOCK, D), lambda i, m: (i, 0, 0)),
            pl.BlockSpec((1, QROWS, HEAD), lambda i, m: (i, 0, 0)),
            pl.BlockSpec((1, KROWS, HEAD), lambda i, m: (i, 0, 0)),
            pl.BlockSpec((1, KROWS, HEAD), lambda i, m: (i, 0, 0)),
        ],
        out_specs=[pl.BlockSpec(shape, lambda i, m: (0, 0, 0, 0, 0))] * 2,
        scratch_shapes=[pltpu.VMEM((3 * HEAD, D), F32)],
    )
    return pl.pallas_call(
        weight_kernel,
        grid_spec=grid_spec,
        out_shape=[jax.ShapeDtypeStruct(shape, BF16)] * 2,
        name="weight_pass",
    )(meta, normed, dq, dk, dv)


def join_kernel(meta, keep, came, out):
    half = meta[NBLK + 1]
    out[:, pl.ds(pl.multiple_of(half * HALF, HALF), HALF), :] = keep[:, 0:HALF, :]
    out[:, pl.ds(pl.multiple_of((1 - half) * HALF, HALF), HALF), :] = came[:, 0:HALF, :]
    both = keep[:, HALF:, :].astype(F32) + came[:, HALF:, :].astype(F32)
    out[:, BLOCK:, :] = both.astype(BF16)


def join_pass(meta, keep, came):
    shape = (8, HALF + 2 * BLOCK, HEAD)
    made = (8, 3 * BLOCK, HEAD)
    grid_spec = pltpu.PrefetchScalarGridSpec(
        num_scalar_prefetch=1,
        grid=(1,),
        in_specs=[pl.BlockSpec(shape, lambda i, m: (0, 0, 0))] * 2,
        out_specs=pl.BlockSpec(made, lambda i, m: (0, 0, 0)),
    )
    return pl.pallas_call(
        join_kernel, grid_spec=grid_spec, out_shape=jax.ShapeDtypeStruct(made, BF16), name="join_pass"
    )(meta, keep, came)


def rows_kernel(back, mine, gain, w, out, grad, d_norm):
    step = pl.program_id(0)

    @pl.when(step == 0)
    def _():
        for h in range(HEADS):
            for n in range(3):
                to = n * D + h * HEAD
                grad[:, to : to + HEAD] = back[h, n * BLOCK : (n + 1) * BLOCK, :]

    d_norm[step] = dot(grad[...], w[...], 1, 1)

    @pl.when(step == STEPS - 1)
    def _():
        values = mine[...].astype(F32)
        inverse = lax.rsqrt(jnp.mean(values * values, axis=-1, keepdims=True) + EPS)
        unit = values * inverse
        gained = jnp.concatenate([d_norm[n] for n in range(STEPS)], axis=1) * gain[...]
        shared = jnp.mean(gained * unit, axis=-1, keepdims=True)
        out[...] = (inverse * (gained - unit * shared)).astype(BF16)


def rows_pass(back, mine, gain, w_qkv):
    return pl.pallas_call(
        rows_kernel,
        grid=(STEPS,),
        in_specs=[
            pl.BlockSpec((HEADS, 3 * BLOCK, HEAD), lambda i: (0, 0, 0)),
            pl.BlockSpec((BLOCK, D), lambda i: (0, 0)),
            pl.BlockSpec((1, D), lambda i: (0, 0)),
            pl.BlockSpec((D // STEPS, 3 * D), lambda i: (i, 0)),
        ],
        out_specs=pl.BlockSpec((BLOCK, D), lambda i: (0, 0)),
        scratch_shapes=[
            pltpu.VMEM((BLOCK, 3 * D), BF16),
            pltpu.VMEM((STEPS, BLOCK, D // STEPS), F32),
        ],
        out_shape=jax.ShapeDtypeStruct((BLOCK, D), BF16),
        name="rows_pass",
    )(back, mine, gain, w_qkv)


def final_kernel(meta, *refs):
    items, out = refs[:4], refs[4]
    half = meta[NBLK + 1]
    x = meta[NBLK + 3]
    for k in range(4):
        source = (x + 4 - k) % 4
        for j in range(2):
            side = half if j == 0 else 1 - half
            row = pl.multiple_of(side * 32 + source * 8, 8)
            for h in range(HEADS):
                for n in range(3):
                    value = items[k][j, h, :, n * HEAD : (n + 1) * HEAD].astype(F32)
                    out[pl.ds(row, 8), n * D + h * HEAD : n * D + (h + 1) * HEAD] = value * (1.0 / math.sqrt(32768))


def final_pass(meta, items):
    shape = (2, HEADS, 8, 3 * HEAD)
    grid_spec = pltpu.PrefetchScalarGridSpec(
        num_scalar_prefetch=1,
        grid=(1,),
        in_specs=[pl.BlockSpec(shape, lambda i, m: (0, 0, 0, 0))] * 4,
        out_specs=pl.BlockSpec((64, 3 * D), lambda i, m: (0, 0)),
    )
    return pl.pallas_call(
        final_kernel, grid_spec=grid_spec, out_shape=jax.ShapeDtypeStruct((64, 3 * D), F32), name="final_pass"
    )(meta, *items)


def flip(x, axis, bit, size):
    return lax.ppermute(x, axis, [(i, i ^ bit) for i in range(size)])


def ring(x, axis, by, size):
    return lax.ppermute(x, axis, [(i, (i + by) % size) for i in range(size)])


def turn(x, by=0):
    pairs = []
    for y in range(2):
        for z in range(8):
            for c in range(2):
                pairs.append(((y * 8 + z) * 2 + c, (c * 8 + (z + by) % 8) * 2 + y))
    return lax.ppermute(x, ("y_lo", "z", "core"), pairs)


def added(a, b):
    return (a.astype(F32) + b.astype(F32)).astype(BF16)


def relay(payload):
    home = turn(payload)
    down, up = turn(payload, -1), turn(payload, 1)
    made = [home, down, up]
    for _ in range(2):
        down, up = ring(down, "z", -1, 8), ring(up, "z", 1, 8)
        made += [down, up]
    made.append(ring(up[:HALF], "z", 1, 8))
    made.append(ring(down[HALF:], "z", -1, 8))
    return made


def body(layer_rows, doc_ids, packing, norm_gain, w_qkv, d_attn):
    z = lax.axis_index("z")
    y = lax.axis_index("y_lo")
    x = lax.axis_index("x")
    core = lax.axis_index("core")
    halves = doc_ids[0].astype(BF16).reshape(2, 1, HALF)
    at = (jnp.arange(4, dtype=jnp.int32) == z % 4).astype(BF16)[None, :, None]
    info = jnp.pad((halves * at).reshape(2, QROWS), ((0, EXTRA - 2), (0, D - QROWS)))
    payload = jnp.concatenate([layer_rows[0], info], axis=0)
    order = turn(packing[0])
    parts = d_attn[0].reshape(2, HALF, HEADS, HEAD).transpose(2, 0, 1, 3)
    parts = turn(parts.reshape(NBLK, HALF, HEAD))
    meta = jnp.concatenate([order, jnp.stack([z, core, y, x]).astype(jnp.int32)])
    gain = norm_gain[None, :]

    pieces = relay(payload)
    others = [flip(piece, "core", 1, 2) for piece in pieces]
    do = lax.all_to_all(parts, ("z", "core"), 0, 0, tiled=True)
    normed, mine, keep, send, dq, dk, dv = head_pass(meta, pieces, others, do, gain, w_qkv)

    came = flip(send, "core", 1, 2)
    back = join_pass(meta, keep, came)
    back = lax.all_to_all(back, "z", 0, 0, tiled=True)

    dwk, dws = weight_pass(meta, normed, dq, dk, dv)
    w_sum = added(dwk, flip(dws, "core", 1, 2))
    w_sum = added(w_sum[0], flip(w_sum[1], "y_lo", 1, 2))
    shares = [lax.dynamic_index_in_dim(w_sum, (x + k) % 4, 0, False) for k in range(4)]
    total = shares[0].astype(F32)
    for k in range(1, 4):
        total = total + ring(shares[k], "x", k, 4).astype(F32)
    w_sum = total.astype(BF16)
    w_sum = added(w_sum, flip(w_sum, "y_hi", 1, 2))
    w_sum = lax.all_to_all(w_sum, "z", 0, 0, tiled=True)
    w_sum = jnp.stack([w_sum, flip(w_sum, "core", 1, 2)])
    w_grad = final_pass(meta, [w_sum] + [ring(w_sum, "x", k, 4) for k in range(1, 4)])

    d_rows = turn(rows_pass(back, mine, gain, w_qkv))
    return (d_rows[None], w_grad)


def solution(mesh):
    fine = Mesh(
        mesh.devices.reshape(2, 8, 4, 2, 2), ("y_lo", "z", "x", "y_hi", "core")
    )
    seq = ("y_lo", "z")
    dp = ("x", "y_hi", "core")
    return jax.shard_map(
        body,
        mesh=fine,
        in_specs=(
            P(dp, seq, None),
            P(dp, seq),
            P(dp, None),
            P(),
            P(),
            P(dp, seq, None),
        ),
        out_specs=(P(dp, seq, None), P(seq, None)),
        check_vma=False,
    )
```

```python
import math

import jax
import jax.numpy as jnp
from jax import lax
from jax.experimental import pallas as pl
from jax.experimental.pallas import tpu as pltpu
from jax.sharding import Mesh
from jax.sharding import PartitionSpec as P

HEADS = 8
HEAD = 128
BLOCK = 128
HALF = 64
NBLK = 16
D = 1024
STEPS = 4
QROWS = 256
KROWS = 512
EXTRA = 8
FACTOR = 1.0 / math.sqrt(HEAD)
EPS = 1e-05
F32 = jnp.float32
BF16 = jnp.bfloat16


def dot(a, b, ca, cb):
    return lax.dot_general(a, b, (((ca,), (cb,)), ((), ())), preferred_element_type=F32)


def place_of(p):
    return (p % 8) * 2 + p // 8


PIECES = 9


def head_kernel(*refs):
    meta, pieces, others, rest = refs[0], refs[1 : 1 + PIECES], refs[1 + PIECES : 1 + 2 * PIECES], refs[1 + 2 * PIECES :]
    (
        do, gain, wq, wk, wv,
        normed, mine, part,
        rows_s, q_s, do_s, k_s, v_s, dk_s, dv_s, e_s, p_s, docs, inv, sems,
    ) = rest
    step = pl.program_id(0)
    z = meta[NBLK]
    half = meta[NBLK + 1]

    @pl.when(step == 0)
    def _():
        copies = []
        for c, group in enumerate((pieces, others)):
            side = half if c == 0 else 1 - half
            for n, ref in enumerate(group):
                offset = (0, 1, 7, 2, 6, 3, 5, 4, 4)[n]
                target = rows_s.at[side * 8 + (z + offset) % 8]
                if n == 7:
                    target = target.at[0:HALF]
                elif n == 8:
                    target = target.at[HALF : BLOCK + EXTRA]
                copies.append(pltpu.make_async_copy(ref, target, sems.at[c * PIECES + n]))
        for copy in copies:
            copy.start()

        def put(p, carry):
            inv[meta[p]] = p
            return carry

        lax.fori_loop(0, NBLK, put, 0)
        docs[...] = jnp.full(docs.shape, 1000.0, F32)
        dk_s[...] = jnp.zeros(dk_s.shape, F32)
        dv_s[...] = jnp.zeros(dv_s.shape, F32)
        for copy in copies:
            copy.wait()
        mine[...] = rows_s[meta[half * 8 + z], 0:BLOCK, :]

    rows = rows_s[pl.ds(step * 4, 4), 0:BLOCK, :].astype(F32)
    inverse = lax.rsqrt(jnp.mean(rows * rows, axis=-1, keepdims=True) + EPS)
    nrm = (rows * inverse * gain[...][None]).astype(BF16)
    normed[...] = nrm
    nrm = nrm.reshape(KROWS, D)
    k_s[step] = dot(nrm, wk[...], 1, 0).astype(BF16)
    v_s[step] = dot(nrm, wv[...], 1, 0).astype(BF16)
    own = pl.multiple_of(half * HALF, HALF)
    qn = normed[:, pl.ds(own, HALF), :].reshape(QROWS, D)
    q_s[...] = dot(qn, wq[...], 1, 0).astype(BF16)
    for t in range(4):
        do_s[t * HALF : (t + 1) * HALF, :] = do[place_of(inv[step * 4 + t])]

    info = jnp.sum(rows_s[pl.ds(step * 4, 4), BLOCK : BLOCK + EXTRA, 0:QROWS].astype(F32), axis=0)
    docs[step] = info
    mine_docs = jnp.where(half == 0, info[0:1, :], info[1:2, :])
    lane = lax.broadcasted_iota(jnp.int32, (1, QROWS), 1)
    q_pos = step * KROWS + (lane // HALF) * BLOCK + half * HALF + lane % HALF
    known = docs[...]
    real = lax.broadcasted_iota(jnp.int32, known.shape, 1) < 2
    first = jnp.zeros((1, QROWS), F32)
    for number in range(1, 6):
        below = jnp.sum(jnp.where((known < number) & real, 1.0, 0.0))
        first = first + jnp.where(mine_docs == number, below, 0.0)
    q_first = first.astype(jnp.int32)

    def scores(g, total):
        s = dot(k_s[g], q_s[...], 1, 1) * FACTOR
        j = g * KROWS + lax.broadcasted_iota(jnp.int32, (KROWS, QROWS), 0)
        e = jnp.where((j >= q_first) & (j <= q_pos), jnp.exp(s), 0.0)
        e_s[g] = e
        return total + jnp.sum(e, axis=0, keepdims=True)

    total = lax.fori_loop(0, step + 1, scores, jnp.zeros((1, QROWS), F32))
    scale = 1.0 / total

    def deltas(g, delta):
        grad = dot(v_s[g], do_s[...], 1, 1)
        p_s[g] = grad
        low = (e_s[g] * scale).astype(BF16)
        dv_s[g] += dot(low, do_s[...], 1, 0)
        return delta + jnp.sum(low.astype(F32) * grad, axis=0, keepdims=True)

    delta = lax.fori_loop(0, step + 1, deltas, jnp.zeros((1, QROWS), F32))

    def grads(g, dq):
        ds = (e_s[g] * scale * (p_s[g] - delta)).astype(BF16)
        dk_s[g] += dot(ds, q_s[...], 1, 0)
        return dq + dot(ds, k_s[g], 0, 0)

    dq = lax.fori_loop(0, step + 1, grads, jnp.zeros((QROWS, HEAD), F32))
    dq = (dq * FACTOR).astype(BF16)
    part[pl.ds(step * 4, 4), 0:HALF, :] = dq.reshape(4, HALF, HEAD)

    @pl.when(step == STEPS - 1)
    def _():
        part[:, HALF : HALF + BLOCK, :] = (dk_s[...] * FACTOR).astype(BF16).reshape(NBLK, BLOCK, HEAD)
        part[:, HALF + BLOCK :, :] = dv_s[...].astype(BF16).reshape(NBLK, BLOCK, HEAD)


def head_pass(meta, pieces, others, do, gain, w_qkv):
    pack = (NBLK, HALF + 2 * BLOCK, HEAD)
    grid_spec = pltpu.PrefetchScalarGridSpec(
        num_scalar_prefetch=1,
        grid=(STEPS,),
        in_specs=[pl.BlockSpec(memory_space=pl.ANY)] * (2 * PIECES)
        + [
            pl.BlockSpec((NBLK, HALF, HEAD), lambda i, m: (0, 0, 0)),
            pl.BlockSpec((1, D), lambda i, m: (0, 0)),
            pl.BlockSpec((D, HEAD), lambda i, m: (0, m[NBLK])),
            pl.BlockSpec((D, HEAD), lambda i, m: (0, HEADS + m[NBLK])),
            pl.BlockSpec((D, HEAD), lambda i, m: (0, 2 * HEADS + m[NBLK])),
        ],
        out_specs=[
            pl.BlockSpec((4, BLOCK, D), lambda i, m: (i, 0, 0)),
            pl.BlockSpec((BLOCK, D), lambda i, m: (0, 0)),
            pl.BlockSpec(pack, lambda i, m: (0, 0, 0)),
        ],
        scratch_shapes=[
            pltpu.VMEM((NBLK, BLOCK + EXTRA, D), BF16),
            pltpu.VMEM((QROWS, HEAD), BF16),
            pltpu.VMEM((QROWS, HEAD), BF16),
            pltpu.VMEM((STEPS, KROWS, HEAD), BF16),
            pltpu.VMEM((STEPS, KROWS, HEAD), BF16),
            pltpu.VMEM((STEPS, KROWS, HEAD), F32),
            pltpu.VMEM((STEPS, KROWS, HEAD), F32),
            pltpu.VMEM((STEPS, KROWS, QROWS), F32),
            pltpu.VMEM((STEPS, KROWS, QROWS), F32),
            pltpu.VMEM((STEPS, EXTRA, QROWS), F32),
            pltpu.SMEM((NBLK,), jnp.int32),
            pltpu.SemaphoreType.DMA((2 * PIECES,)),
        ],
    )
    return pl.pallas_call(
        head_kernel,
        grid_spec=grid_spec,
        out_shape=[
            jax.ShapeDtypeStruct((NBLK, BLOCK, D), BF16),
            jax.ShapeDtypeStruct((BLOCK, D), BF16),
            jax.ShapeDtypeStruct(pack, BF16),
        ],
        name="head_pass",
    )(meta, *pieces, *others, do, gain, w_qkv, w_qkv, w_qkv)


def total_of(part, came, half, blocks):
    low = part[blocks, 0:HALF, :]
    high = came[blocks, 0:HALF, :]
    first = jnp.where(half == 0, low, high)
    second = jnp.where(half == 0, high, low)
    both = part[blocks, HALF:, :].astype(F32) + came[blocks, HALF:, :].astype(F32)
    return first, second, both.astype(BF16)


def weight_kernel(meta, normed, part, came, here, there, dw_s):
    step = pl.program_id(0)
    half = meta[NBLK + 1]
    y = meta[NBLK + 2]
    first, second, both = total_of(part, came, half, slice(None))
    dq = jnp.concatenate([first, second], axis=1).reshape(KROWS, HEAD)
    dk = both[:, 0:BLOCK, :].reshape(KROWS, HEAD)
    dv = both[:, BLOCK:, :].reshape(KROWS, HEAD)
    grads = jnp.concatenate([dq, dk, dv], axis=1)
    made = dot(normed[...].reshape(KROWS, D // 2), grads, 0, 0)

    @pl.when(step == 0)
    def _():
        dw_s[...] = made

    @pl.when(step > 0)
    def _():
        dw_s[...] += made

    @pl.when(step == STEPS - 1)
    def _():
        every = dw_s[...].reshape(8, 2, 32, 3 * HEAD)
        here[...] = jnp.where(y == 0, every[:, 0], every[:, 1]).astype(BF16)
        there[...] = jnp.where(y == 0, every[:, 1], every[:, 0]).astype(BF16)


def weight_pass(meta, normed, part, came):
    pack = (4, HALF + 2 * BLOCK, HEAD)
    shape = (8, 32, 3 * HEAD)
    grid_spec = pltpu.PrefetchScalarGridSpec(
        num_scalar_prefetch=1,
        grid=(STEPS,),
        in_specs=[
            pl.BlockSpec((4, BLOCK, D // 2), lambda i, m: (i, 0, m[NBLK + 1])),
            pl.BlockSpec(pack, lambda i, m: (i, 0, 0)),
            pl.BlockSpec(pack, lambda i, m: (i, 0, 0)),
        ],
        out_specs=[pl.BlockSpec(shape, lambda i, m: (0, 0, 0))] * 2,
        scratch_shapes=[pltpu.VMEM((D // 2, 3 * HEAD), F32)],
    )
    return pl.pallas_call(
        weight_kernel,
        grid_spec=grid_spec,
        out_shape=[jax.ShapeDtypeStruct(shape, BF16)] * 2,
        name="weight_pass",
    )(meta, normed, part, came)


def join_kernel(meta, part, came, out):
    half = meta[NBLK + 1]
    for n in range(8):
        first, second, both = total_of(part, came, half, meta[half * 8 + n])
        out[n, 0:HALF, :] = first
        out[n, HALF:BLOCK, :] = second
        out[n, BLOCK:, :] = both


def join_pass(meta, part, came):
    shape = (NBLK, HALF + 2 * BLOCK, HEAD)
    made = (8, 3 * BLOCK, HEAD)
    grid_spec = pltpu.PrefetchScalarGridSpec(
        num_scalar_prefetch=1,
        grid=(1,),
        in_specs=[pl.BlockSpec(shape, lambda i, m: (0, 0, 0))] * 2,
        out_specs=pl.BlockSpec(made, lambda i, m: (0, 0, 0)),
    )
    return pl.pallas_call(
        join_kernel, grid_spec=grid_spec, out_shape=jax.ShapeDtypeStruct(made, BF16), name="join_pass"
    )(meta, part, came)


def rows_kernel(back, mine, gain, w, out, grad, d_norm):
    step = pl.program_id(0)

    @pl.when(step == 0)
    def _():
        for h in range(HEADS):
            for n in range(3):
                to = n * D + h * HEAD
                grad[:, to : to + HEAD] = back[h, n * BLOCK : (n + 1) * BLOCK, :]

    d_norm[pl.ds(pl.multiple_of(step * 256, 256), 256), :] = dot(w[...], grad[...], 1, 1)

    @pl.when(step == STEPS - 1)
    def _():
        values = mine[...].astype(F32)
        inverse = lax.rsqrt(jnp.mean(values * values, axis=-1, keepdims=True) + EPS)
        unit = values * inverse
        gained = d_norm[...].T * gain[...]
        shared = jnp.mean(gained * unit, axis=-1, keepdims=True)
        out[...] = (inverse * (gained - unit * shared)).astype(BF16)


def rows_pass(back, mine, gain, w_qkv):
    return pl.pallas_call(
        rows_kernel,
        grid=(STEPS,),
        in_specs=[
            pl.BlockSpec((HEADS, 3 * BLOCK, HEAD), lambda i: (0, 0, 0)),
            pl.BlockSpec((BLOCK, D), lambda i: (0, 0)),
            pl.BlockSpec((1, D), lambda i: (0, 0)),
            pl.BlockSpec((D // STEPS, 3 * D), lambda i: (i, 0)),
        ],
        out_specs=pl.BlockSpec((BLOCK, D), lambda i: (0, 0)),
        scratch_shapes=[
            pltpu.VMEM((BLOCK, 3 * D), BF16),
            pltpu.VMEM((D, BLOCK), F32),
        ],
        out_shape=jax.ShapeDtypeStruct((BLOCK, D), BF16),
        name="rows_pass",
    )(back, mine, gain, w_qkv)


def final_kernel(meta, own, other, out):
    half = meta[NBLK + 1]
    for side, ref in ((half, own), (1 - half, other)):
        row = pl.multiple_of(side * 32, 32)
        for h in range(HEADS):
            for n in range(3):
                value = ref[h, :, n * HEAD : (n + 1) * HEAD].astype(F32)
                out[pl.ds(row, 32), n * D + h * HEAD : n * D + (h + 1) * HEAD] = value * (1.0 / math.sqrt(32768))


def final_pass(meta, own, other):
    shape = (HEADS, 32, 3 * HEAD)
    grid_spec = pltpu.PrefetchScalarGridSpec(
        num_scalar_prefetch=1,
        grid=(1,),
        in_specs=[pl.BlockSpec(shape, lambda i, m: (0, 0, 0))] * 2,
        out_specs=pl.BlockSpec((64, 3 * D), lambda i, m: (0, 0)),
    )
    return pl.pallas_call(
        final_kernel, grid_spec=grid_spec, out_shape=jax.ShapeDtypeStruct((64, 3 * D), F32), name="final_pass"
    )(meta, own, other)


def flip(x, axis, bit, size):
    return lax.ppermute(x, axis, [(i, i ^ bit) for i in range(size)])


def ring(x, axis, by, size):
    return lax.ppermute(x, axis, [(i, (i + by) % size) for i in range(size)])


def turn(x, by=0, other=0):
    pairs = []
    for y in range(2):
        for z in range(8):
            for c in range(2):
                pairs.append(((y * 8 + z) * 2 + c, (c * 8 + (z + by) % 8) * 2 + (y ^ other)))
    return lax.ppermute(x, ("y_lo", "z", "core"), pairs)


def added(a, b):
    return (a.astype(F32) + b.astype(F32)).astype(BF16)


def relay(payload):
    home = turn(payload)
    down, up = turn(payload, -1), turn(payload, 1)
    made = [home, down, up]
    for _ in range(2):
        down, up = ring(down, "z", -1, 8), ring(up, "z", 1, 8)
        made += [down, up]
    made.append(ring(up[:HALF], "z", 1, 8))
    made.append(ring(down[HALF:], "z", -1, 8))
    return made


def work(layer_rows, doc_ids, packing, norm_gain, w_qkv, d_attn):
    z = lax.axis_index("z")
    y = lax.axis_index("y_lo")
    x = lax.axis_index("x")
    core = lax.axis_index("core")
    halves = doc_ids[0].astype(BF16).reshape(2, 1, HALF)
    at = (jnp.arange(4, dtype=jnp.int32) == z % 4).astype(BF16)[None, :, None]
    info = jnp.pad((halves * at).reshape(2, QROWS), ((0, EXTRA - 2), (0, D - QROWS)))
    payload = jnp.concatenate([layer_rows[0], info], axis=0)
    order = turn(packing[0])
    parts = d_attn[0].reshape(2, HALF, HEADS, HEAD).transpose(2, 0, 1, 3)
    parts = turn(parts.reshape(NBLK, HALF, HEAD))
    meta = jnp.concatenate([order, jnp.stack([z, core, y, x]).astype(jnp.int32)])
    gain = norm_gain[None, :]

    pieces = relay(payload)
    others = [flip(piece, "core", 1, 2) for piece in pieces]
    do = lax.all_to_all(parts, ("z", "core"), 0, 0, tiled=True)
    normed, mine, part = head_pass(meta, pieces, others, do, gain, w_qkv)
    came = flip(part, "core", 1, 2)
    here, there = weight_pass(meta, normed, part, came)
    back = join_pass(meta, part, came)
    back = lax.all_to_all(back, "z", 0, 0, tiled=True)

    here = turn(here)
    there = turn(there, 0, 1)
    w_sum = added(here, there)
    w_sum = added(w_sum, flip(w_sum, "x", 1, 4))
    w_sum = added(w_sum, flip(w_sum, "x", 2, 4))
    w_sum = added(w_sum, flip(w_sum, "y_hi", 1, 2))
    w_sum = lax.all_to_all(w_sum, "z", 0, 0, tiled=True)
    other = flip(w_sum, "core", 1, 2)
    w_grad = final_pass(meta, w_sum, other)

    d_rows = rows_pass(back, mine, gain, w_qkv)
    d_rows = turn(d_rows)
    return (d_rows[None], w_grad)


def solution(mesh):
    fine = Mesh(
        mesh.devices.reshape(2, 8, 4, 2, 2), ("y_lo", "z", "x", "y_hi", "core")
    )
    seq = ("y_lo", "z")
    dp = ("x", "y_hi", "core")
    return jax.shard_map(
        work,
        mesh=fine,
        in_specs=(
            P(dp, seq, None),
            P(dp, seq),
            P(dp, None),
            P(),
            P(),
            P(dp, seq, None),
        ),
        out_specs=(P(dp, seq, None), P(seq, None)),
        check_vma=False,
    )
```

```python
import math

import jax
import jax.numpy as jnp
from jax import lax
from jax.experimental import pallas as pl
from jax.experimental.pallas import tpu as pltpu
from jax.sharding import Mesh
from jax.sharding import PartitionSpec as P

HEADS = 8
HEAD = 128
BLOCK = 128
HALF = 64
NBLK = 16
D = 1024
STEPS = 4
QROWS = 256
KROWS = 512
EXTRA = 8
FACTOR = 1.0 / math.sqrt(HEAD)
EPS = 1e-05
F32 = jnp.float32
BF16 = jnp.bfloat16


def dot(a, b, ca, cb):
    return lax.dot_general(a, b, (((ca,), (cb,)), ((), ())), preferred_element_type=F32)


def place_of(p):
    return (p % 8) * 2 + p // 8


PIECES = 9


def head_kernel(*refs):
    meta, pieces, others, rest = refs[0], refs[1 : 1 + PIECES], refs[1 + PIECES : 1 + 2 * PIECES], refs[1 + 2 * PIECES :]
    (
        do, gain, wq, wk, wv,
        normed, mine, part,
        rows_s, q_s, do_s, k_s, v_s, dk_s, dv_s, e_s, p_s, docs, inv, sems,
    ) = rest
    step = pl.program_id(0)
    z = meta[NBLK]
    half = meta[NBLK + 1]

    @pl.when(step == 0)
    def _():
        copies = []
        for c, group in enumerate((pieces, others)):
            side = half if c == 0 else 1 - half
            for n, ref in enumerate(group):
                offset = (0, 1, 7, 2, 6, 3, 5, 4, 4)[n]
                target = rows_s.at[side * 8 + (z + offset) % 8]
                if n == 7:
                    target = target.at[0:HALF]
                elif n == 8:
                    target = target.at[HALF : BLOCK + EXTRA]
                copies.append(pltpu.make_async_copy(ref, target, sems.at[c * PIECES + n]))
        for copy in copies:
            copy.start()

        def put(p, carry):
            inv[meta[p]] = p
            return carry

        lax.fori_loop(0, NBLK, put, 0)
        docs[...] = jnp.full(docs.shape, 1000.0, F32)
        dk_s[...] = jnp.zeros(dk_s.shape, F32)
        dv_s[...] = jnp.zeros(dv_s.shape, F32)
        for copy in copies:
            copy.wait()
        mine[...] = rows_s[meta[half * 8 + z], 0:BLOCK, :]

    rows = rows_s[pl.ds(step * 4, 4), 0:BLOCK, :].astype(F32)
    inverse = lax.rsqrt(jnp.mean(rows * rows, axis=-1, keepdims=True) + EPS)
    nrm = (rows * inverse * gain[...][None]).astype(BF16)
    normed[...] = nrm
    nrm = nrm.reshape(KROWS, D)
    k_s[step] = dot(nrm, wk[...], 1, 0).astype(BF16)
    v_s[step] = dot(nrm, wv[...], 1, 0).astype(BF16)
    own = pl.multiple_of(half * HALF, HALF)
    qn = normed[:, pl.ds(own, HALF), :].reshape(QROWS, D)
    q_s[...] = dot(qn, wq[...], 1, 0).astype(BF16)
    for t in range(4):
        do_s[t * HALF : (t + 1) * HALF, :] = do[place_of(inv[step * 4 + t])]

    info = jnp.sum(rows_s[pl.ds(step * 4, 4), BLOCK : BLOCK + EXTRA, 0:QROWS].astype(F32), axis=0)
    docs[step] = info
    mine_docs = jnp.where(half == 0, info[0:1, :], info[1:2, :])
    lane = lax.broadcasted_iota(jnp.int32, (1, QROWS), 1)
    q_pos = step * KROWS + (lane // HALF) * BLOCK + half * HALF + lane % HALF
    known = docs[...]
    real = lax.broadcasted_iota(jnp.int32, known.shape, 1) < 2
    first = jnp.zeros((1, QROWS), F32)
    for number in range(1, 6):
        below = jnp.sum(jnp.where((known < number) & real, 1.0, 0.0))
        first = first + jnp.where(mine_docs == number, below, 0.0)
    q_first = first.astype(jnp.int32)

    def scores(g, total):
        s = dot(k_s[g], q_s[...], 1, 1) * FACTOR
        j = g * KROWS + lax.broadcasted_iota(jnp.int32, (KROWS, QROWS), 0)
        e = jnp.where((j >= q_first) & (j <= q_pos), jnp.exp(s), 0.0)
        e_s[g] = e
        return total + jnp.sum(e, axis=0, keepdims=True)

    total = lax.fori_loop(0, step + 1, scores, jnp.zeros((1, QROWS), F32))
    scale = 1.0 / total

    def deltas(g, delta):
        grad = dot(v_s[g], do_s[...], 1, 1)
        p_s[g] = grad
        low = (e_s[g] * scale).astype(BF16)
        dv_s[g] += dot(low, do_s[...], 1, 0)
        return delta + jnp.sum(low.astype(F32) * grad, axis=0, keepdims=True)

    delta = lax.fori_loop(0, step + 1, deltas, jnp.zeros((1, QROWS), F32))

    def grads(g, dq):
        ds = (e_s[g] * scale * (p_s[g] - delta)).astype(BF16)
        dk_s[g] += dot(ds, q_s[...], 1, 0)
        return dq + dot(ds, k_s[g], 0, 0)

    dq = lax.fori_loop(0, step + 1, grads, jnp.zeros((QROWS, HEAD), F32))
    dq = (dq * FACTOR).astype(BF16)
    part[pl.ds(step * 4, 4), 0:HALF, :] = dq.reshape(4, HALF, HEAD)

    @pl.when(step == STEPS - 1)
    def _():
        part[:, HALF : HALF + BLOCK, :] = (dk_s[...] * FACTOR).astype(BF16).reshape(NBLK, BLOCK, HEAD)
        part[:, HALF + BLOCK :, :] = dv_s[...].astype(BF16).reshape(NBLK, BLOCK, HEAD)


def head_pass(meta, pieces, others, do, gain, w_qkv):
    pack = (NBLK, HALF + 2 * BLOCK, HEAD)
    grid_spec = pltpu.PrefetchScalarGridSpec(
        num_scalar_prefetch=1,
        grid=(STEPS,),
        in_specs=[pl.BlockSpec(memory_space=pl.ANY)] * (2 * PIECES)
        + [
            pl.BlockSpec((NBLK, HALF, HEAD), lambda i, m: (0, 0, 0)),
            pl.BlockSpec((1, D), lambda i, m: (0, 0)),
            pl.BlockSpec((D, HEAD), lambda i, m: (0, m[NBLK])),
            pl.BlockSpec((D, HEAD), lambda i, m: (0, HEADS + m[NBLK])),
            pl.BlockSpec((D, HEAD), lambda i, m: (0, 2 * HEADS + m[NBLK])),
        ],
        out_specs=[
            pl.BlockSpec((4, BLOCK, D), lambda i, m: (i, 0, 0)),
            pl.BlockSpec((BLOCK, D), lambda i, m: (0, 0)),
            pl.BlockSpec(pack, lambda i, m: (0, 0, 0)),
        ],
        scratch_shapes=[
            pltpu.VMEM((NBLK, BLOCK + EXTRA, D), BF16),
            pltpu.VMEM((QROWS, HEAD), BF16),
            pltpu.VMEM((QROWS, HEAD), BF16),
            pltpu.VMEM((STEPS, KROWS, HEAD), BF16),
            pltpu.VMEM((STEPS, KROWS, HEAD), BF16),
            pltpu.VMEM((STEPS, KROWS, HEAD), F32),
            pltpu.VMEM((STEPS, KROWS, HEAD), F32),
            pltpu.VMEM((STEPS, KROWS, QROWS), F32),
            pltpu.VMEM((STEPS, KROWS, QROWS), F32),
            pltpu.VMEM((STEPS, EXTRA, QROWS), F32),
            pltpu.SMEM((NBLK,), jnp.int32),
            pltpu.SemaphoreType.DMA((2 * PIECES,)),
        ],
    )
    return pl.pallas_call(
        head_kernel,
        grid_spec=grid_spec,
        out_shape=[
            jax.ShapeDtypeStruct((NBLK, BLOCK, D), BF16),
            jax.ShapeDtypeStruct((BLOCK, D), BF16),
            jax.ShapeDtypeStruct(pack, BF16),
        ],
        name="head_pass", compiler_params=pltpu.CompilerParams(vmem_limit_bytes=26 * 1024 * 1024),
    )(meta, *pieces, *others, do, gain, w_qkv, w_qkv, w_qkv)


def total_of(part, came, half, blocks):
    low = part[blocks, 0:HALF, :]
    high = came[blocks, 0:HALF, :]
    first = jnp.where(half == 0, low, high)
    second = jnp.where(half == 0, high, low)
    both = part[blocks, HALF:, :].astype(F32) + came[blocks, HALF:, :].astype(F32)
    return first, second, both.astype(BF16)


def weight_kernel(meta, normed, part, came, here, there, dw_s):
    step = pl.program_id(0)
    half = meta[NBLK + 1]
    y = meta[NBLK + 2]
    first, second, both = total_of(part, came, half, slice(None))
    dq = jnp.concatenate([first, second], axis=1).reshape(KROWS, HEAD)
    dk = both[:, 0:BLOCK, :].reshape(KROWS, HEAD)
    dv = both[:, BLOCK:, :].reshape(KROWS, HEAD)
    grads = jnp.concatenate([dq, dk, dv], axis=1)
    made = dot(normed[...].reshape(KROWS, D // 2), grads, 0, 0)

    @pl.when(step == 0)
    def _():
        dw_s[...] = made

    @pl.when(step > 0)
    def _():
        dw_s[...] += made

    @pl.when(step == STEPS - 1)
    def _():
        every = dw_s[...].reshape(8, 2, 32, 3 * HEAD)
        here[...] = jnp.where(y == 0, every[:, 0], every[:, 1]).astype(BF16)
        there[...] = jnp.where(y == 0, every[:, 1], every[:, 0]).astype(BF16)


def weight_pass(meta, normed, part, came):
    pack = (4, HALF + 2 * BLOCK, HEAD)
    shape = (8, 32, 3 * HEAD)
    grid_spec = pltpu.PrefetchScalarGridSpec(
        num_scalar_prefetch=1,
        grid=(STEPS,),
        in_specs=[
            pl.BlockSpec((4, BLOCK, D // 2), lambda i, m: (i, 0, m[NBLK + 1])),
            pl.BlockSpec(pack, lambda i, m: (i, 0, 0)),
            pl.BlockSpec(pack, lambda i, m: (i, 0, 0)),
        ],
        out_specs=[pl.BlockSpec(shape, lambda i, m: (0, 0, 0))] * 2,
        scratch_shapes=[pltpu.VMEM((D // 2, 3 * HEAD), F32)],
    )
    return pl.pallas_call(
        weight_kernel,
        grid_spec=grid_spec,
        out_shape=[jax.ShapeDtypeStruct(shape, BF16)] * 2,
        name="weight_pass", compiler_params=pltpu.CompilerParams(vmem_limit_bytes=10 * 1024 * 1024),
    )(meta, normed, part, came)


def join_kernel(meta, part, came, out):
    half = meta[NBLK + 1]
    for n in range(8):
        first, second, both = total_of(part, came, half, meta[half * 8 + n])
        out[n, 0:HALF, :] = first
        out[n, HALF:BLOCK, :] = second
        out[n, BLOCK:, :] = both


def join_pass(meta, part, came):
    shape = (NBLK, HALF + 2 * BLOCK, HEAD)
    made = (8, 3 * BLOCK, HEAD)
    grid_spec = pltpu.PrefetchScalarGridSpec(
        num_scalar_prefetch=1,
        grid=(1,),
        in_specs=[pl.BlockSpec(shape, lambda i, m: (0, 0, 0))] * 2,
        out_specs=pl.BlockSpec(made, lambda i, m: (0, 0, 0)),
    )
    return pl.pallas_call(
        join_kernel, grid_spec=grid_spec, out_shape=jax.ShapeDtypeStruct(made, BF16), name="join_pass", compiler_params=pltpu.CompilerParams(vmem_limit_bytes=10 * 1024 * 1024)
    )(meta, part, came)


def rows_kernel(back, mine, gain, w, out, grad, d_norm):
    step = pl.program_id(0)

    @pl.when(step == 0)
    def _():
        for h in range(HEADS):
            for n in range(3):
                to = n * D + h * HEAD
                grad[:, to : to + HEAD] = back[h, n * BLOCK : (n + 1) * BLOCK, :]

    d_norm[pl.ds(pl.multiple_of(step * 256, 256), 256), :] = dot(w[...], grad[...], 1, 1)

    @pl.when(step == STEPS - 1)
    def _():
        values = mine[...].astype(F32)
        inverse = lax.rsqrt(jnp.mean(values * values, axis=-1, keepdims=True) + EPS)
        unit = values * inverse
        gained = d_norm[...].T * gain[...]
        shared = jnp.mean(gained * unit, axis=-1, keepdims=True)
        out[...] = (inverse * (gained - unit * shared)).astype(BF16)


def rows_pass(back, mine, gain, w_qkv):
    return pl.pallas_call(
        rows_kernel,
        grid=(STEPS,),
        in_specs=[
            pl.BlockSpec((HEADS, 3 * BLOCK, HEAD), lambda i: (0, 0, 0)),
            pl.BlockSpec((BLOCK, D), lambda i: (0, 0)),
            pl.BlockSpec((1, D), lambda i: (0, 0)),
            pl.BlockSpec((D // STEPS, 3 * D), lambda i: (i, 0)),
        ],
        out_specs=pl.BlockSpec((BLOCK, D), lambda i: (0, 0)),
        scratch_shapes=[
            pltpu.VMEM((BLOCK, 3 * D), BF16),
            pltpu.VMEM((D, BLOCK), F32),
        ],
        out_shape=jax.ShapeDtypeStruct((BLOCK, D), BF16),
        name="rows_pass", compiler_params=pltpu.CompilerParams(vmem_limit_bytes=12 * 1024 * 1024),
    )(back, mine, gain, w_qkv)


def final_kernel(meta, own, other, out):
    half = meta[NBLK + 1]
    for side, ref in ((half, own), (1 - half, other)):
        row = pl.multiple_of(side * 32, 32)
        for h in range(HEADS):
            for n in range(3):
                value = ref[h, :, n * HEAD : (n + 1) * HEAD].astype(F32)
                out[pl.ds(row, 32), n * D + h * HEAD : n * D + (h + 1) * HEAD] = value * (1.0 / math.sqrt(32768))


def final_pass(meta, own, other):
    shape = (HEADS, 32, 3 * HEAD)
    grid_spec = pltpu.PrefetchScalarGridSpec(
        num_scalar_prefetch=1,
        grid=(1,),
        in_specs=[pl.BlockSpec(shape, lambda i, m: (0, 0, 0))] * 2,
        out_specs=pl.BlockSpec((64, 3 * D), lambda i, m: (0, 0)),
    )
    return pl.pallas_call(
        final_kernel, grid_spec=grid_spec, out_shape=jax.ShapeDtypeStruct((64, 3 * D), F32), name="final_pass", compiler_params=pltpu.CompilerParams(vmem_limit_bytes=6 * 1024 * 1024)
    )(meta, own, other)


def flip(x, axis, bit, size):
    return lax.ppermute(x, axis, [(i, i ^ bit) for i in range(size)])


def ring(x, axis, by, size):
    return lax.ppermute(x, axis, [(i, (i + by) % size) for i in range(size)])


def turn(x, by=0, other=0):
    pairs = []
    for y in range(2):
        for z in range(8):
            for c in range(2):
                pairs.append(((y * 8 + z) * 2 + c, (c * 8 + (z + by) % 8) * 2 + (y ^ other)))
    return lax.ppermute(x, ("y_lo", "z", "core"), pairs)


def added(a, b):
    return (a.astype(F32) + b.astype(F32)).astype(BF16)


def relay(payload):
    home = turn(payload)
    down, up = turn(payload, -1), turn(payload, 1)
    made = [home, down, up]
    for _ in range(2):
        down, up = ring(down, "z", -1, 8), ring(up, "z", 1, 8)
        made += [down, up]
    made.append(ring(up[:HALF], "z", 1, 8))
    made.append(ring(down[HALF:], "z", -1, 8))
    return made


def work(layer_rows, doc_ids, packing, norm_gain, w_qkv, d_attn):
    z = lax.axis_index("z")
    y = lax.axis_index("y_lo")
    x = lax.axis_index("x")
    core = lax.axis_index("core")
    halves = doc_ids[0].astype(BF16).reshape(2, 1, HALF)
    at = (jnp.arange(4, dtype=jnp.int32) == z % 4).astype(BF16)[None, :, None]
    info = jnp.pad((halves * at).reshape(2, QROWS), ((0, EXTRA - 2), (0, D - QROWS)))
    payload = jnp.concatenate([layer_rows[0], info], axis=0)
    order = turn(packing[0])
    parts = d_attn[0].reshape(2, HALF, HEADS, HEAD).transpose(2, 0, 1, 3)
    parts = turn(parts.reshape(NBLK, HALF, HEAD))
    meta = jnp.concatenate([order, jnp.stack([z, core, y, x]).astype(jnp.int32)])
    gain = norm_gain[None, :]

    pieces = relay(payload)
    others = [flip(piece, "core", 1, 2) for piece in pieces]
    do = lax.all_to_all(parts, ("z", "core"), 0, 0, tiled=True)
    normed, mine, part = head_pass(meta, pieces, others, do, gain, w_qkv)
    came = flip(part, "core", 1, 2)
    here, there = weight_pass(meta, normed, part, came)
    back = join_pass(meta, part, came)
    back = lax.all_to_all(back, "z", 0, 0, tiled=True)

    here = turn(here)
    there = turn(there, 0, 1)
    w_sum = added(here, there)
    w_sum = added(w_sum, flip(w_sum, "x", 1, 4))
    w_sum = added(w_sum, flip(w_sum, "x", 2, 4))
    w_sum = added(w_sum, flip(w_sum, "y_hi", 1, 2))
    w_sum = lax.all_to_all(w_sum, "z", 0, 0, tiled=True)
    other = flip(w_sum, "core", 1, 2)
    w_grad = final_pass(meta, w_sum, other)

    d_rows = rows_pass(back, mine, gain, w_qkv)
    d_rows = turn(d_rows)
    return (d_rows[None], w_grad)


def solution(mesh):
    fine = Mesh(
        mesh.devices.reshape(2, 8, 4, 2, 2), ("y_lo", "z", "x", "y_hi", "core")
    )
    seq = ("y_lo", "z")
    dp = ("x", "y_hi", "core")
    return jax.shard_map(
        work,
        mesh=fine,
        in_specs=(
            P(dp, seq, None),
            P(dp, seq),
            P(dp, None),
            P(),
            P(),
            P(dp, seq, None),
        ),
        out_specs=(P(dp, seq, None), P(seq, None)),
        check_vma=False,
    )
```

```python
import math

import jax
import jax.numpy as jnp
from jax import lax
from jax.experimental import pallas as pl
from jax.experimental.pallas import tpu as pltpu
from jax.sharding import Mesh
from jax.sharding import PartitionSpec as P

HEADS = 8
HEAD = 128
BLOCK = 128
HALF = 64
NBLK = 16
D = 1024
STEPS = 4
QROWS = 256
KROWS = 512
EXTRA = 8
FACTOR = 1.0 / math.sqrt(HEAD)
EPS = 1e-05
F32 = jnp.float32
BF16 = jnp.bfloat16


def dot(a, b, ca, cb):
    return lax.dot_general(a, b, (((ca,), (cb,)), ((), ())), preferred_element_type=F32)


def place_of(p):
    return (p % 8) * 2 + p // 8


PIECES = 9


def head_kernel(*refs):
    meta, pieces, others, rest = refs[0], refs[1 : 1 + PIECES], refs[1 + PIECES : 1 + 2 * PIECES], refs[1 + 2 * PIECES :]
    (
        do, gain, wq, wk, wv,
        normed, mine, part,
        rows_s, q_s, do_s, k_s, v_s, dk_s, dv_s, e_s, p_s, docs, inv, sems,
    ) = rest
    step = pl.program_id(0)
    z = meta[NBLK]
    half = meta[NBLK + 1]

    @pl.when(step == 0)
    def _():
        copies = []
        for c, group in enumerate((pieces, others)):
            side = half if c == 0 else 1 - half
            for n, ref in enumerate(group):
                offset = (0, 1, 7, 2, 6, 3, 5, 4, 4)[n]
                target = rows_s.at[side * 8 + (z + offset) % 8]
                if n == 7:
                    target = target.at[0:HALF]
                elif n == 8:
                    target = target.at[HALF : BLOCK + EXTRA]
                copies.append(pltpu.make_async_copy(ref, target, sems.at[c * PIECES + n]))
        for copy in copies:
            copy.start()

        def put(p, carry):
            inv[meta[p]] = p
            return carry

        lax.fori_loop(0, NBLK, put, 0)
        docs[...] = jnp.full(docs.shape, 1000.0, F32)
        dk_s[...] = jnp.zeros(dk_s.shape, F32)
        dv_s[...] = jnp.zeros(dv_s.shape, F32)
        for copy in copies:
            copy.wait()
        mine[...] = rows_s[meta[half * 8 + z], 0:BLOCK, :]

    rows = rows_s[pl.ds(step * 4, 4), 0:BLOCK, :].astype(F32)
    inverse = lax.rsqrt(jnp.mean(rows * rows, axis=-1, keepdims=True) + EPS)
    nrm = (rows * inverse * gain[0:1, :][None]).astype(BF16)
    normed[...] = nrm
    nrm = nrm.reshape(KROWS, D)
    k_s[step] = dot(nrm, wk[...], 1, 0).astype(BF16)
    v_s[step] = dot(nrm, wv[...], 1, 0).astype(BF16)
    own = pl.multiple_of(half * HALF, HALF)
    qn = normed[:, pl.ds(own, HALF), :].reshape(QROWS, D)
    q_s[...] = dot(qn, wq[...], 1, 0).astype(BF16)
    for t in range(4):
        do_s[t * HALF : (t + 1) * HALF, :] = do[place_of(inv[step * 4 + t])]

    info = jnp.sum(rows_s[pl.ds(step * 4, 4), BLOCK : BLOCK + EXTRA, 0:QROWS].astype(F32), axis=0)
    docs[step] = info
    mine_docs = jnp.where(half == 0, info[0:1, :], info[1:2, :])
    lane = lax.broadcasted_iota(jnp.int32, (1, QROWS), 1)
    q_pos = step * KROWS + (lane // HALF) * BLOCK + half * HALF + lane % HALF
    known = docs[...]
    real = lax.broadcasted_iota(jnp.int32, known.shape, 1) < 2
    first = jnp.zeros((1, QROWS), F32)
    for number in range(1, 6):
        below = jnp.sum(jnp.where((known < number) & real, 1.0, 0.0))
        first = first + jnp.where(mine_docs == number, below, 0.0)
    q_first = first.astype(jnp.int32)
    low_tile = jnp.min(q_first) // KROWS

    def scores(g, total):
        s = dot(k_s[g], q_s[...], 1, 1) * FACTOR
        j = g * KROWS + lax.broadcasted_iota(jnp.int32, (KROWS, QROWS), 0)
        e = jnp.where((j >= q_first) & (j <= q_pos), jnp.exp(s), 0.0)
        e_s[g] = e
        return total + jnp.sum(e, axis=0, keepdims=True)

    total = lax.fori_loop(low_tile, step + 1, scores, jnp.zeros((1, QROWS), F32))
    scale = 1.0 / total

    def deltas(g, delta):
        grad = dot(v_s[g], do_s[...], 1, 1)
        p_s[g] = grad
        low = (e_s[g] * scale).astype(BF16)
        dv_s[g] += dot(low, do_s[...], 1, 0)
        return delta + jnp.sum(low.astype(F32) * grad, axis=0, keepdims=True)

    delta = lax.fori_loop(low_tile, step + 1, deltas, jnp.zeros((1, QROWS), F32))

    def grads(g, dq):
        ds = (e_s[g] * scale * (p_s[g] - delta)).astype(BF16)
        dk_s[g] += dot(ds, q_s[...], 1, 0)
        return dq + dot(ds, k_s[g], 0, 0)

    dq = lax.fori_loop(low_tile, step + 1, grads, jnp.zeros((QROWS, HEAD), F32))
    dq = (dq * FACTOR).astype(BF16)
    part[pl.ds(step * 4, 4), 0:HALF, :] = dq.reshape(4, HALF, HEAD)

    @pl.when(step == STEPS - 1)
    def _():
        part[:, HALF : HALF + BLOCK, :] = (dk_s[...] * FACTOR).astype(BF16).reshape(NBLK, BLOCK, HEAD)
        part[:, HALF + BLOCK :, :] = dv_s[...].astype(BF16).reshape(NBLK, BLOCK, HEAD)


def head_pass(meta, pieces, others, do, gain, w_head):
    pack = (NBLK, HALF + 2 * BLOCK, HEAD)
    grid_spec = pltpu.PrefetchScalarGridSpec(
        num_scalar_prefetch=1,
        grid=(STEPS,),
        in_specs=[pl.BlockSpec(memory_space=pl.ANY)] * (2 * PIECES)
        + [
            pl.BlockSpec((NBLK, HALF, HEAD), lambda i, m: (0, 0, 0)),
            pl.BlockSpec((8, D), lambda i, m: (0, 0)),
        ]
        + [pl.BlockSpec((D, HEAD), lambda i, m: (0, 0))] * 3,
        out_specs=[
            pl.BlockSpec((4, BLOCK, D), lambda i, m: (i, 0, 0)),
            pl.BlockSpec((BLOCK, D), lambda i, m: (0, 0)),
            pl.BlockSpec(pack, lambda i, m: (0, 0, 0)),
        ],
        scratch_shapes=[
            pltpu.VMEM((NBLK, BLOCK + EXTRA, D), BF16),
            pltpu.VMEM((QROWS, HEAD), BF16),
            pltpu.VMEM((QROWS, HEAD), BF16),
            pltpu.VMEM((STEPS, KROWS, HEAD), BF16),
            pltpu.VMEM((STEPS, KROWS, HEAD), BF16),
            pltpu.VMEM((STEPS, KROWS, HEAD), F32),
            pltpu.VMEM((STEPS, KROWS, HEAD), F32),
            pltpu.VMEM((STEPS, KROWS, QROWS), F32),
            pltpu.VMEM((STEPS, KROWS, QROWS), F32),
            pltpu.VMEM((STEPS, EXTRA, QROWS), F32),
            pltpu.SMEM((NBLK,), jnp.int32),
            pltpu.SemaphoreType.DMA((2 * PIECES,)),
        ],
    )
    return pl.pallas_call(
        head_kernel,
        grid_spec=grid_spec,
        out_shape=[
            jax.ShapeDtypeStruct((NBLK, BLOCK, D), BF16),
            jax.ShapeDtypeStruct((BLOCK, D), BF16),
            jax.ShapeDtypeStruct(pack, BF16),
        ],
        name="head_pass", compiler_params=pltpu.CompilerParams(vmem_limit_bytes=26 * 1024 * 1024),
    )(meta, *pieces, *others, do, gain, *w_head)


def total_of(part, came, half, blocks):
    low = part[blocks, 0:HALF, :]
    high = came[blocks, 0:HALF, :]
    first = jnp.where(half == 0, low, high)
    second = jnp.where(half == 0, high, low)
    both = part[blocks, HALF:, :].astype(F32) + came[blocks, HALF:, :].astype(F32)
    return first, second, both.astype(BF16)


def weight_kernel(meta, normed, part, came, here, there, dw_s):
    step = pl.program_id(0)
    half = meta[NBLK + 1]
    y = meta[NBLK + 2]
    first, second, both = total_of(part, came, half, slice(None))
    dq = jnp.concatenate([first, second], axis=1).reshape(KROWS, HEAD)
    dk = both[:, 0:BLOCK, :].reshape(KROWS, HEAD)
    dv = both[:, BLOCK:, :].reshape(KROWS, HEAD)
    grads = jnp.concatenate([dq, dk, dv], axis=1)
    made = dot(normed[...].reshape(KROWS, D // 2), grads, 0, 0)

    @pl.when(step == 0)
    def _():
        dw_s[...] = made

    @pl.when(step > 0)
    def _():
        dw_s[...] += made

    @pl.when(step == STEPS - 1)
    def _():
        every = dw_s[...].reshape(8, 2, 32, 3 * HEAD)
        here[...] = jnp.where(y == 0, every[:, 0], every[:, 1]).astype(BF16)
        there[...] = jnp.where(y == 0, every[:, 1], every[:, 0]).astype(BF16)


def weight_pass(meta, normed, part, came):
    pack = (4, HALF + 2 * BLOCK, HEAD)
    shape = (8, 32, 3 * HEAD)
    grid_spec = pltpu.PrefetchScalarGridSpec(
        num_scalar_prefetch=1,
        grid=(STEPS,),
        in_specs=[
            pl.BlockSpec((4, BLOCK, D // 2), lambda i, m: (i, 0, m[NBLK + 1])),
            pl.BlockSpec(pack, lambda i, m: (i, 0, 0)),
            pl.BlockSpec(pack, lambda i, m: (i, 0, 0)),
        ],
        out_specs=[pl.BlockSpec(shape, lambda i, m: (0, 0, 0))] * 2,
        scratch_shapes=[pltpu.VMEM((D // 2, 3 * HEAD), F32)],
    )
    return pl.pallas_call(
        weight_kernel,
        grid_spec=grid_spec,
        out_shape=[jax.ShapeDtypeStruct(shape, BF16)] * 2,
        name="weight_pass", compiler_params=pltpu.CompilerParams(vmem_limit_bytes=10 * 1024 * 1024),
    )(meta, normed, part, came)


def join_kernel(meta, part, came, out):
    half = meta[NBLK + 1]
    for n in range(8):
        first, second, both = total_of(part, came, half, meta[half * 8 + n])
        out[n, 0:HALF, :] = first
        out[n, HALF:BLOCK, :] = second
        out[n, BLOCK:, :] = both


def join_pass(meta, part, came):
    shape = (NBLK, HALF + 2 * BLOCK, HEAD)
    made = (8, 3 * BLOCK, HEAD)
    grid_spec = pltpu.PrefetchScalarGridSpec(
        num_scalar_prefetch=1,
        grid=(1,),
        in_specs=[pl.BlockSpec(shape, lambda i, m: (0, 0, 0))] * 2,
        out_specs=pl.BlockSpec(made, lambda i, m: (0, 0, 0)),
    )
    return pl.pallas_call(
        join_kernel, grid_spec=grid_spec, out_shape=jax.ShapeDtypeStruct(made, BF16), name="join_pass", compiler_params=pltpu.CompilerParams(vmem_limit_bytes=10 * 1024 * 1024)
    )(meta, part, came)


def rows_kernel(back, mine, gain, w, out, grad, d_norm):
    step = pl.program_id(0)

    @pl.when(step == 0)
    def _():
        for h in range(HEADS):
            for n in range(3):
                to = n * D + h * HEAD
                grad[:, to : to + HEAD] = back[h, n * BLOCK : (n + 1) * BLOCK, :]

    d_norm[pl.ds(pl.multiple_of(step * 256, 256), 256), :] = dot(w[...], grad[...], 1, 1)

    @pl.when(step == STEPS - 1)
    def _():
        values = mine[...].astype(F32)
        inverse = lax.rsqrt(jnp.mean(values * values, axis=-1, keepdims=True) + EPS)
        unit = values * inverse
        gained = d_norm[...].T * gain[0:1, :]
        shared = jnp.mean(gained * unit, axis=-1, keepdims=True)
        out[...] = (inverse * (gained - unit * shared)).astype(BF16)


def rows_pass(back, mine, gain, w_qkv):
    return pl.pallas_call(
        rows_kernel,
        grid=(STEPS,),
        in_specs=[
            pl.BlockSpec((HEADS, 3 * BLOCK, HEAD), lambda i: (0, 0, 0)),
            pl.BlockSpec((BLOCK, D), lambda i: (0, 0)),
            pl.BlockSpec((8, D), lambda i: (0, 0)),
            pl.BlockSpec((D // STEPS, 3 * D), lambda i: (i, 0)),
        ],
        out_specs=pl.BlockSpec((BLOCK, D), lambda i: (0, 0)),
        scratch_shapes=[
            pltpu.VMEM((BLOCK, 3 * D), BF16),
            pltpu.VMEM((D, BLOCK), F32),
        ],
        out_shape=jax.ShapeDtypeStruct((BLOCK, D), BF16),
        name="rows_pass", compiler_params=pltpu.CompilerParams(vmem_limit_bytes=12 * 1024 * 1024),
    )(back, mine, gain, w_qkv)


def final_kernel(meta, own, other, out):
    half = meta[NBLK + 1]
    for side, ref in ((half, own), (1 - half, other)):
        row = pl.multiple_of(side * 32, 32)
        for h in range(HEADS):
            for n in range(3):
                value = ref[h, :, n * HEAD : (n + 1) * HEAD].astype(F32)
                out[pl.ds(row, 32), n * D + h * HEAD : n * D + (h + 1) * HEAD] = value * (1.0 / math.sqrt(32768))


def final_pass(meta, own, other):
    shape = (HEADS, 32, 3 * HEAD)
    grid_spec = pltpu.PrefetchScalarGridSpec(
        num_scalar_prefetch=1,
        grid=(1,),
        in_specs=[pl.BlockSpec(shape, lambda i, m: (0, 0, 0))] * 2,
        out_specs=pl.BlockSpec((64, 3 * D), lambda i, m: (0, 0)),
    )
    return pl.pallas_call(
        final_kernel, grid_spec=grid_spec, out_shape=jax.ShapeDtypeStruct((64, 3 * D), F32), name="final_pass", compiler_params=pltpu.CompilerParams(vmem_limit_bytes=6 * 1024 * 1024)
    )(meta, own, other)


def flip(x, axis, bit, size):
    return lax.ppermute(x, axis, [(i, i ^ bit) for i in range(size)])


def ring(x, axis, by, size):
    return lax.ppermute(x, axis, [(i, (i + by) % size) for i in range(size)])


def turn(x, by=0, other=0):
    pairs = []
    for y in range(2):
        for z in range(8):
            for c in range(2):
                pairs.append(((y * 8 + z) * 2 + c, (c * 8 + (z + by) % 8) * 2 + (y ^ other)))
    return lax.ppermute(x, ("y_lo", "z", "core"), pairs)


def added(a, b):
    return (a.astype(F32) + b.astype(F32)).astype(BF16)


def relay(payload):
    home = turn(payload)
    down, up = turn(payload, -1), turn(payload, 1)
    made = [home, down, up]
    for _ in range(2):
        down, up = ring(down, "z", -1, 8), ring(up, "z", 1, 8)
        made += [down, up]
    far = ring(up[:HALF], "z", 1, 8)
    made.append(far)
    made.append(ring(down[HALF:], "z", -1, 8))
    return made


def work(layer_rows, doc_ids, packing, norm_gain, w_qkv, d_attn):
    z = lax.axis_index("z")
    y = lax.axis_index("y_lo")
    x = lax.axis_index("x")
    core = lax.axis_index("core")
    halves = doc_ids[0].astype(BF16).reshape(2, 1, HALF)
    at = (jnp.arange(4, dtype=jnp.int32) == z % 4).astype(BF16)[None, :, None]
    info = jnp.pad((halves * at).reshape(2, QROWS), ((0, EXTRA - 2), (0, D - QROWS)))
    payload = jnp.concatenate([layer_rows[0], info], axis=0)
    order = turn(packing[0])
    parts = d_attn[0].reshape(2, HALF, HEADS, HEAD).transpose(2, 0, 1, 3)
    parts = turn(parts.reshape(NBLK, HALF, HEAD))
    meta = jnp.concatenate([order, jnp.stack([z, core, y, x]).astype(jnp.int32)])
    gain = jnp.broadcast_to(norm_gain[None, :], (8, D))
    w_head = [lax.dynamic_slice_in_dim(w_qkv, n * D + z * HEAD, HEAD, 1) for n in range(3)]

    pieces = relay(payload)
    others = [flip(piece, "core", 1, 2) for piece in pieces]
    do = lax.all_to_all(parts, ("z", "core"), 0, 0, tiled=True)
    normed, mine, part = head_pass(meta, pieces, others, do, gain, w_head)
    came = flip(part, "core", 1, 2)
    here, there = weight_pass(meta, normed, part, came)
    back = join_pass(meta, part, came)
    back = lax.all_to_all(back, "z", 0, 0, tiled=True)

    here = turn(here)
    there = turn(there, 0, 1)
    w_sum = added(here, there)
    w_sum = added(w_sum, flip(w_sum, "x", 1, 4))
    w_sum = added(w_sum, flip(w_sum, "x", 2, 4))
    w_sum = added(w_sum, flip(w_sum, "y_hi", 1, 2))
    w_sum = lax.all_to_all(w_sum, "z", 0, 0, tiled=True)
    other = flip(w_sum, "core", 1, 2)
    w_grad = final_pass(meta, w_sum, other)

    d_rows = rows_pass(back, mine, gain, w_qkv)
    d_rows = turn(d_rows)
    return (d_rows[None], w_grad)


def solution(mesh):
    fine = Mesh(
        mesh.devices.reshape(2, 8, 4, 2, 2), ("y_lo", "z", "x", "y_hi", "core")
    )
    seq = ("y_lo", "z")
    dp = ("x", "y_hi", "core")
    return jax.shard_map(
        work,
        mesh=fine,
        in_specs=(
            P(dp, seq, None),
            P(dp, seq),
            P(dp, None),
            P(),
            P(),
            P(dp, seq, None),
        ),
        out_specs=(P(dp, seq, None), P(seq, None)),
        check_vma=False,
    )
```

```python
import math

import jax
import jax.numpy as jnp
from jax import lax
from jax.experimental import pallas as pl
from jax.experimental.pallas import tpu as pltpu
from jax.sharding import Mesh
from jax.sharding import PartitionSpec as P

HEADS = 8
HEAD = 128
BLOCK = 128
HALF = 64
NBLK = 16
D = 1024
STEPS = 4
QROWS = 256
KROWS = 512
EXTRA = 8
FACTOR = 1.0 / math.sqrt(HEAD)
EPS = 1e-05
F32 = jnp.float32
BF16 = jnp.bfloat16


def dot(a, b, ca, cb):
    return lax.dot_general(a, b, (((ca,), (cb,)), ((), ())), preferred_element_type=F32)


def place_of(p):
    return (p % 8) * 2 + p // 8


EARLY = (0, 1, 7, 2, 6)
LATE = (3, 5, 4)


def block_at(meta, n, offsets):
    half = meta[NBLK + 1]
    side = half if n < len(offsets) else 1 - half
    return side * 8 + (meta[NBLK] + offsets[n % len(offsets)]) % 8


def project(meta, n, rows, gain, wq, wk, wv, normed):
    values = rows.astype(F32)
    inverse = lax.rsqrt(jnp.mean(values * values, axis=-1, keepdims=True) + EPS)
    nrm = (values * inverse * gain[0:1, :]).astype(BF16)
    normed[n : n + 2] = nrm.reshape(2, BLOCK, D)
    own = pl.multiple_of(meta[NBLK + 1] * HALF, HALF)
    qn = normed[n : n + 2, pl.ds(own, HALF), :].reshape(BLOCK, D)
    q = dot(qn, wq[...], 1, 0).astype(BF16).reshape(2, HALF, HEAD)
    k = dot(nrm, wk[...], 1, 0).astype(BF16).reshape(2, BLOCK, HEAD)
    v = dot(nrm, wv[...], 1, 0).astype(BF16).reshape(2, BLOCK, HEAD)
    return q, k, v


def early_kernel(*refs):
    meta, pieces = refs[0], refs[1:11]
    gain, wq, wk, wv, normed, q_o, k_o, v_o, info, mine = refs[11:]
    target = meta[meta[NBLK + 1] * 8 + meta[NBLK]]
    mine[...] = jnp.zeros(mine.shape, BF16)
    for n in range(0, 10, 2):
        rows = jnp.concatenate([pieces[n][0:BLOCK, :], pieces[n + 1][0:BLOCK, :]], axis=0)
        q_o[n : n + 2], k_o[n : n + 2], v_o[n : n + 2] = project(meta, n, rows, gain, wq, wk, wv, normed)
    for n in range(10):
        info[n] = pieces[n][BLOCK : BLOCK + EXTRA, 0:QROWS].astype(F32)

        @pl.when(block_at(meta, n, EARLY) == target)
        def _():
            mine[...] = pieces[n][0:BLOCK, :]


def early_pass(meta, pieces, gain, w_head):
    made = [
        ((10, BLOCK, D), BF16),
        ((10, HALF, HEAD), BF16),
        ((10, BLOCK, HEAD), BF16),
        ((10, BLOCK, HEAD), BF16),
        ((10, EXTRA, QROWS), F32),
        ((BLOCK, D), BF16),
    ]
    return pl.pallas_call(
        early_kernel,
        grid_spec=pltpu.PrefetchScalarGridSpec(
            num_scalar_prefetch=1,
            grid=(1,),
            in_specs=[pl.BlockSpec((BLOCK + EXTRA, D), lambda i, m: (0, 0))] * 10
            + [pl.BlockSpec((8, D), lambda i, m: (0, 0))]
            + [pl.BlockSpec((D, HEAD), lambda i, m: (0, 0))] * 3,
            out_specs=[pl.BlockSpec(x, lambda i, m, r=len(x): (0,) * r) for x, t in made],
        ),
        out_shape=[jax.ShapeDtypeStruct(x, t) for x, t in made],
        name="early_pass",
        compiler_params=pltpu.CompilerParams(vmem_limit_bytes=20 * 1024 * 1024),
    )(meta, *pieces, gain, *w_head)


def head_kernel(*refs):
    meta, pieces = refs[0], refs[1:9]
    (
        q_i, k_i, v_i, info_i, mine_i, do, gain, wq, wk, wv,
        normed, mine, part,
        q_s, do_s, k_s, v_s, dk_s, dv_s, e_s, p_s, docs, inv,
    ) = refs[9:]
    step = pl.program_id(0)
    half = meta[NBLK + 1]

    @pl.when(step == 0)
    def _():
        def put(p, carry):
            inv[meta[p]] = p
            return carry

        lax.fori_loop(0, NBLK, put, 0)
        docs[...] = jnp.zeros(docs.shape, F32)
        dk_s[...] = jnp.zeros(dk_s.shape, F32)
        dv_s[...] = jnp.zeros(dv_s.shape, F32)
        mine[...] = mine_i[...]
        for n in range(10):
            b = block_at(meta, n, EARLY)
            q_s[b] = q_i[n]
            k_s[b] = k_i[n]
            v_s[b] = v_i[n]
            docs[b // 4] += info_i[n]
        raw = []
        for c in range(2):
            down, up, top, low = pieces[c * 4 : c * 4 + 4]
            raw.append((down[0:BLOCK, :], down[BLOCK : BLOCK + EXTRA, 0:QROWS]))
            raw.append((up[0:BLOCK, :], up[BLOCK : BLOCK + EXTRA, 0:QROWS]))
            raw.append((jnp.concatenate([top[...], low[0:HALF, :]], axis=0), low[HALF : HALF + EXTRA, 0:QROWS]))
        target = meta[half * 8 + meta[NBLK]]
        for n in range(0, 6, 2):
            rows = jnp.concatenate([raw[n][0], raw[n + 1][0]], axis=0)
            q, k, v = project(meta, n, rows, gain, wq, wk, wv, normed)
            for i in range(2):
                b = block_at(meta, n + i, LATE)
                q_s[b] = q[i]
                k_s[b] = k[i]
                v_s[b] = v[i]
                docs[b // 4] += raw[n + i][1].astype(F32)

                @pl.when(b == target)
                def _():
                    mine[...] = raw[n + i][0]

    q = q_s[pl.ds(step * 4, 4)].reshape(QROWS, HEAD)
    for t in range(4):
        do_s[t * HALF : (t + 1) * HALF, :] = do[place_of(inv[step * 4 + t])]
    info = docs[step]
    mine_docs = jnp.where(half == 0, info[0:1, :], info[1:2, :])
    lane = lax.broadcasted_iota(jnp.int32, (1, QROWS), 1)
    q_pos = step * KROWS + (lane // HALF) * BLOCK + half * HALF + lane % HALF
    known = docs[...]
    real = lax.broadcasted_iota(jnp.int32, known.shape, 1) < 2
    first = jnp.zeros((1, QROWS), F32)
    for number in range(1, 6):
        below = jnp.sum(jnp.where((known < number) & real, 1.0, 0.0))
        first = first + jnp.where(mine_docs == number, below, 0.0)
    q_first = first.astype(jnp.int32)
    low_tile = jnp.min(q_first) // KROWS

    def scores(g, total):
        s = dot(k_s[pl.ds(g * 4, 4)].reshape(KROWS, HEAD), q, 1, 1) * FACTOR
        j = g * KROWS + lax.broadcasted_iota(jnp.int32, (KROWS, QROWS), 0)
        e = jnp.where((j >= q_first) & (j <= q_pos), jnp.exp(s), 0.0)
        e_s[g] = e
        return total + jnp.sum(e, axis=0, keepdims=True)

    total = lax.fori_loop(low_tile, step + 1, scores, jnp.zeros((1, QROWS), F32))
    scale = 1.0 / total

    def deltas(g, delta):
        grad = dot(v_s[pl.ds(g * 4, 4)].reshape(KROWS, HEAD), do_s[...], 1, 1)
        p_s[g] = grad
        low = (e_s[g] * scale).astype(BF16)
        dv_s[g] += dot(low, do_s[...], 1, 0)
        return delta + jnp.sum(low.astype(F32) * grad, axis=0, keepdims=True)

    delta = lax.fori_loop(low_tile, step + 1, deltas, jnp.zeros((1, QROWS), F32))

    def grads(g, dq):
        ds = (e_s[g] * scale * (p_s[g] - delta)).astype(BF16)
        dk_s[g] += dot(ds, q, 1, 0)
        return dq + dot(ds, k_s[pl.ds(g * 4, 4)].reshape(KROWS, HEAD), 0, 0)

    dq = lax.fori_loop(low_tile, step + 1, grads, jnp.zeros((QROWS, HEAD), F32))
    dq = (dq * FACTOR).astype(BF16)
    part[pl.ds(step * 4, 4), 0:HALF, :] = dq.reshape(4, HALF, HEAD)

    @pl.when(step == STEPS - 1)
    def _():
        part[:, HALF : HALF + BLOCK, :] = (dk_s[...] * FACTOR).astype(BF16).reshape(NBLK, BLOCK, HEAD)
        part[:, HALF + BLOCK :, :] = dv_s[...].astype(BF16).reshape(NBLK, BLOCK, HEAD)


def head_pass(meta, pieces, made, do, gain, w_head):
    pack = (NBLK, HALF + 2 * BLOCK, HEAD)
    given = [*pieces, *made, do, gain, *w_head]
    outs = [(6, BLOCK, D), (BLOCK, D), pack]
    return pl.pallas_call(
        head_kernel,
        grid_spec=pltpu.PrefetchScalarGridSpec(
            num_scalar_prefetch=1,
            grid=(STEPS,),
            in_specs=[pl.BlockSpec(x.shape, lambda i, m, r=x.ndim: (0,) * r) for x in given],
            out_specs=[pl.BlockSpec(x, lambda i, m, r=len(x): (0,) * r) for x in outs],
            scratch_shapes=[
                pltpu.VMEM((NBLK, HALF, HEAD), BF16),
                pltpu.VMEM((QROWS, HEAD), BF16),
                pltpu.VMEM((NBLK, BLOCK, HEAD), BF16),
                pltpu.VMEM((NBLK, BLOCK, HEAD), BF16),
                pltpu.VMEM((STEPS, KROWS, HEAD), F32),
                pltpu.VMEM((STEPS, KROWS, HEAD), F32),
                pltpu.VMEM((STEPS, KROWS, QROWS), F32),
                pltpu.VMEM((STEPS, KROWS, QROWS), F32),
                pltpu.VMEM((STEPS, EXTRA, QROWS), F32),
                pltpu.SMEM((NBLK,), jnp.int32),
            ],
        ),
        out_shape=[jax.ShapeDtypeStruct(x, BF16) for x in outs],
        name="head_pass",
        compiler_params=pltpu.CompilerParams(vmem_limit_bytes=26 * 1024 * 1024),
    )(meta, *given)


def total_of(part, came, half, blocks):
    low = part[blocks, 0:HALF, :]
    high = came[blocks, 0:HALF, :]
    first = jnp.where(half == 0, low, high)
    second = jnp.where(half == 0, high, low)
    both = part[blocks, HALF:, :].astype(F32) + came[blocks, HALF:, :].astype(F32)
    return first, second, both.astype(BF16)


def weight_kernel(meta, n_early, n_late, part, came, here, there, grads):
    half = meta[NBLK + 1]
    y = meta[NBLK + 2]
    for n in range(NBLK):
        b = block_at(meta, n, EARLY) if n < 10 else block_at(meta, n - 10, LATE)
        first, second, both = total_of(part, came, half, b)
        grads[n, 0:HALF, 0:HEAD] = first
        grads[n, HALF:BLOCK, 0:HEAD] = second
        grads[n, :, HEAD : 2 * HEAD] = both[0:BLOCK]
        grads[n, :, 2 * HEAD :] = both[BLOCK:]
    made = dot(n_early[...].reshape(10 * BLOCK, D // 2), grads[0:10].reshape(10 * BLOCK, 3 * HEAD), 0, 0)
    made = made + dot(n_late[...].reshape(6 * BLOCK, D // 2), grads[10:16].reshape(6 * BLOCK, 3 * HEAD), 0, 0)
    every = made.reshape(8, 2, 32, 3 * HEAD)
    here[...] = jnp.where(y == 0, every[:, 0], every[:, 1]).astype(BF16)
    there[...] = jnp.where(y == 0, every[:, 1], every[:, 0]).astype(BF16)


def weight_pass(meta, n_early, n_late, part, came):
    pack = (NBLK, HALF + 2 * BLOCK, HEAD)
    shape = (8, 32, 3 * HEAD)
    grid_spec = pltpu.PrefetchScalarGridSpec(
        num_scalar_prefetch=1,
        grid=(1,),
        in_specs=[
            pl.BlockSpec((10, BLOCK, D // 2), lambda i, m: (0, 0, m[NBLK + 1])),
            pl.BlockSpec((6, BLOCK, D // 2), lambda i, m: (0, 0, m[NBLK + 1])),
            pl.BlockSpec(pack, lambda i, m: (0, 0, 0)),
            pl.BlockSpec(pack, lambda i, m: (0, 0, 0)),
        ],
        out_specs=[pl.BlockSpec(shape, lambda i, m: (0, 0, 0))] * 2,
        scratch_shapes=[pltpu.VMEM((NBLK, BLOCK, 3 * HEAD), BF16)],
    )
    return pl.pallas_call(
        weight_kernel,
        grid_spec=grid_spec,
        out_shape=[jax.ShapeDtypeStruct(shape, BF16)] * 2,
        name="weight_pass",
        compiler_params=pltpu.CompilerParams(vmem_limit_bytes=18 * 1024 * 1024),
    )(meta, n_early, n_late, part, came)


def join_kernel(meta, part, came, out):
    half = meta[NBLK + 1]
    for n in range(8):
        first, second, both = total_of(part, came, half, meta[half * 8 + n])
        out[n, 0:HALF, :] = first
        out[n, HALF:BLOCK, :] = second
        out[n, BLOCK:, :] = both


def join_pass(meta, part, came):
    shape = (NBLK, HALF + 2 * BLOCK, HEAD)
    made = (8, 3 * BLOCK, HEAD)
    grid_spec = pltpu.PrefetchScalarGridSpec(
        num_scalar_prefetch=1,
        grid=(1,),
        in_specs=[pl.BlockSpec(shape, lambda i, m: (0, 0, 0))] * 2,
        out_specs=pl.BlockSpec(made, lambda i, m: (0, 0, 0)),
    )
    return pl.pallas_call(
        join_kernel, grid_spec=grid_spec, out_shape=jax.ShapeDtypeStruct(made, BF16), name="join_pass", compiler_params=pltpu.CompilerParams(vmem_limit_bytes=10 * 1024 * 1024)
    )(meta, part, came)


def rows_kernel(back, mine, gain, w, out, grad, d_norm):
    step = pl.program_id(0)

    @pl.when(step == 0)
    def _():
        for h in range(HEADS):
            for n in range(3):
                to = n * D + h * HEAD
                grad[:, to : to + HEAD] = back[h, n * BLOCK : (n + 1) * BLOCK, :]

    d_norm[pl.ds(pl.multiple_of(step * 256, 256), 256), :] = dot(w[...], grad[...], 1, 1)

    @pl.when(step == STEPS - 1)
    def _():
        values = mine[...].astype(F32)
        inverse = lax.rsqrt(jnp.mean(values * values, axis=-1, keepdims=True) + EPS)
        unit = values * inverse
        gained = d_norm[...].T * gain[0:1, :]
        shared = jnp.mean(gained * unit, axis=-1, keepdims=True)
        out[...] = (inverse * (gained - unit * shared)).astype(BF16)


def rows_pass(back, mine, gain, w_qkv):
    return pl.pallas_call(
        rows_kernel,
        grid=(STEPS,),
        in_specs=[
            pl.BlockSpec((HEADS, 3 * BLOCK, HEAD), lambda i: (0, 0, 0)),
            pl.BlockSpec((BLOCK, D), lambda i: (0, 0)),
            pl.BlockSpec((8, D), lambda i: (0, 0)),
            pl.BlockSpec((D // STEPS, 3 * D), lambda i: (i, 0)),
        ],
        out_specs=pl.BlockSpec((BLOCK, D), lambda i: (0, 0)),
        scratch_shapes=[
            pltpu.VMEM((BLOCK, 3 * D), BF16),
            pltpu.VMEM((D, BLOCK), F32),
        ],
        out_shape=jax.ShapeDtypeStruct((BLOCK, D), BF16),
        name="rows_pass", compiler_params=pltpu.CompilerParams(vmem_limit_bytes=12 * 1024 * 1024),
    )(back, mine, gain, w_qkv)


def final_kernel(meta, own, other, out):
    half = meta[NBLK + 1]
    for side, ref in ((half, own), (1 - half, other)):
        row = pl.multiple_of(side * 32, 32)
        for h in range(HEADS):
            for n in range(3):
                value = ref[h, :, n * HEAD : (n + 1) * HEAD].astype(F32)
                out[pl.ds(row, 32), n * D + h * HEAD : n * D + (h + 1) * HEAD] = value * (1.0 / math.sqrt(32768))


def final_pass(meta, own, other):
    shape = (HEADS, 32, 3 * HEAD)
    grid_spec = pltpu.PrefetchScalarGridSpec(
        num_scalar_prefetch=1,
        grid=(1,),
        in_specs=[pl.BlockSpec(shape, lambda i, m: (0, 0, 0))] * 2,
        out_specs=pl.BlockSpec((64, 3 * D), lambda i, m: (0, 0)),
    )
    return pl.pallas_call(
        final_kernel, grid_spec=grid_spec, out_shape=jax.ShapeDtypeStruct((64, 3 * D), F32), name="final_pass", compiler_params=pltpu.CompilerParams(vmem_limit_bytes=6 * 1024 * 1024)
    )(meta, own, other)


def flip(x, axis, bit, size):
    return lax.ppermute(x, axis, [(i, i ^ bit) for i in range(size)])


def ring(x, axis, by, size):
    return lax.ppermute(x, axis, [(i, (i + by) % size) for i in range(size)])


def turn(x, by=0, other=0):
    pairs = []
    for y in range(2):
        for z in range(8):
            for c in range(2):
                pairs.append(((y * 8 + z) * 2 + c, (c * 8 + (z + by) % 8) * 2 + (y ^ other)))
    return lax.ppermute(x, ("y_lo", "z", "core"), pairs)


def added(a, b):
    return (a.astype(F32) + b.astype(F32)).astype(BF16)


def relay(payload):
    home = turn(payload)
    down, up = turn(payload, -1), turn(payload, 1)
    made = [home, down, up]
    for _ in range(2):
        down, up = ring(down, "z", -1, 8), ring(up, "z", 1, 8)
        made += [down, up]
    far = ring(up[:HALF], "z", 1, 8)
    made.append(far)
    far = ring(down[HALF:], "z", -1, 8)
    made.append(far)
    return made


def work(layer_rows, doc_ids, packing, norm_gain, w_qkv, d_attn):
    z = lax.axis_index("z")
    y = lax.axis_index("y_lo")
    x = lax.axis_index("x")
    core = lax.axis_index("core")
    halves = doc_ids[0].astype(BF16).reshape(2, 1, HALF)
    at = (jnp.arange(4, dtype=jnp.int32) == z % 4).astype(BF16)[None, :, None]
    info = jnp.pad((halves * at).reshape(2, QROWS), ((0, EXTRA - 2), (0, D - QROWS)))
    payload = jnp.concatenate([layer_rows[0], info], axis=0)
    order = turn(packing[0])
    parts = d_attn[0].reshape(2, HALF, HEADS, HEAD).transpose(2, 0, 1, 3)
    parts = turn(parts.reshape(NBLK, HALF, HEAD))
    meta = jnp.concatenate([order, jnp.stack([z, core, y, x]).astype(jnp.int32)])
    gain = jnp.broadcast_to(norm_gain[None, :], (8, D))
    w_head = [lax.dynamic_slice_in_dim(w_qkv, n * D + z * HEAD, HEAD, 1) for n in range(3)]

    pieces = relay(payload)
    others = [flip(piece, "core", 1, 2) for piece in pieces]
    early, *made = early_pass(meta, pieces[:5] + others[:5], gain, w_head)
    do = lax.all_to_all(parts, ("z", "core"), 0, 0, tiled=True)
    late, mine, part = head_pass(meta, pieces[5:] + others[5:], made, do, gain, w_head)
    came = flip(part, "core", 1, 2)
    here, there = weight_pass(meta, early, late, part, came)
    back = join_pass(meta, part, came)
    back = lax.all_to_all(back, "z", 0, 0, tiled=True)

    here = turn(here)
    there = turn(there, 0, 1)
    w_sum = added(here, there)
    w_sum = added(w_sum, flip(w_sum, "x", 1, 4))
    w_sum = added(w_sum, flip(w_sum, "x", 2, 4))
    w_sum = added(w_sum, flip(w_sum, "y_hi", 1, 2))
    w_sum = lax.all_to_all(w_sum, "z", 0, 0, tiled=True)
    other = flip(w_sum, "core", 1, 2)
    w_grad = final_pass(meta, w_sum, other)

    d_rows = rows_pass(back, mine, gain, w_qkv)
    d_rows = turn(d_rows)
    return (d_rows[None], w_grad)


def solution(mesh):
    fine = Mesh(
        mesh.devices.reshape(2, 8, 4, 2, 2), ("y_lo", "z", "x", "y_hi", "core")
    )
    seq = ("y_lo", "z")
    dp = ("x", "y_hi", "core")
    return jax.shard_map(
        work,
        mesh=fine,
        in_specs=(
            P(dp, seq, None),
            P(dp, seq),
            P(dp, None),
            P(),
            P(),
            P(dp, seq, None),
        ),
        out_specs=(P(dp, seq, None), P(seq, None)),
        check_vma=False,
    )
```

```python
import math

import jax
import jax.numpy as jnp
from jax import lax
from jax.experimental import pallas as pl
from jax.experimental.pallas import tpu as pltpu
from jax.sharding import Mesh
from jax.sharding import PartitionSpec as P

HEADS = 8
HEAD = 128
BLOCK = 128
HALF = 64
NBLK = 16
D = 1024
STEPS = 4
QROWS = 256
KROWS = 512
EXTRA = 8
FACTOR = 1.0 / math.sqrt(HEAD)
EPS = 1e-05
F32 = jnp.float32
BF16 = jnp.bfloat16


def dot(a, b, ca, cb):
    return lax.dot_general(a, b, (((ca,), (cb,)), ((), ())), preferred_element_type=F32)


def place_of(p):
    return (p % 8) * 2 + p // 8


EARLY = (0, 1, 7, 2, 6)
LATE = (3, 5, 4)


def block_at(meta, n, offsets):
    half = meta[NBLK + 1]
    side = half if n < len(offsets) else 1 - half
    return side * 8 + (meta[NBLK] + offsets[n % len(offsets)]) % 8


def project(meta, n, rows, gain, wq, wk, wv, normed):
    values = rows.astype(F32)
    inverse = lax.rsqrt(jnp.mean(values * values, axis=-1, keepdims=True) + EPS)
    nrm = (values * inverse * gain[0:1, :]).astype(BF16)
    normed[n : n + 2] = nrm.reshape(2, BLOCK, D)
    own = pl.multiple_of(meta[NBLK + 1] * HALF, HALF)
    qn = normed[n : n + 2, pl.ds(own, HALF), :].reshape(BLOCK, D)
    q = dot(qn, wq[...], 1, 0).astype(BF16).reshape(2, HALF, HEAD)
    k = dot(nrm, wk[...], 1, 0).astype(BF16).reshape(2, BLOCK, HEAD)
    v = dot(nrm, wv[...], 1, 0).astype(BF16).reshape(2, BLOCK, HEAD)
    return q, k, v


def early_kernel(*refs):
    meta, pieces = refs[0], refs[1:11]
    gain, wq, wk, wv, normed, q_o, k_o, v_o, info, mine = refs[11:]
    target = meta[meta[NBLK + 1] * 8 + meta[NBLK]]
    mine[...] = jnp.zeros(mine.shape, BF16)
    for n in range(0, 10, 2):
        rows = jnp.concatenate([pieces[n][0:BLOCK, :], pieces[n + 1][0:BLOCK, :]], axis=0)
        q_o[n : n + 2], k_o[n : n + 2], v_o[n : n + 2] = project(meta, n, rows, gain, wq, wk, wv, normed)
    for n in range(10):
        info[n] = pieces[n][BLOCK : BLOCK + EXTRA, 0:QROWS].astype(F32)

        @pl.when(block_at(meta, n, EARLY) == target)
        def _():
            mine[...] = pieces[n][0:BLOCK, :]


def early_pass(meta, pieces, gain, w_head):
    made = [
        ((10, BLOCK, D), BF16),
        ((10, HALF, HEAD), BF16),
        ((10, BLOCK, HEAD), BF16),
        ((10, BLOCK, HEAD), BF16),
        ((10, EXTRA, QROWS), F32),
        ((BLOCK, D), BF16),
    ]
    return pl.pallas_call(
        early_kernel,
        grid_spec=pltpu.PrefetchScalarGridSpec(
            num_scalar_prefetch=1,
            grid=(1,),
            in_specs=[pl.BlockSpec((BLOCK + EXTRA, D), lambda i, m: (0, 0))] * 10
            + [pl.BlockSpec((8, D), lambda i, m: (0, 0))]
            + [pl.BlockSpec((D, HEAD), lambda i, m: (0, 0))] * 3,
            out_specs=[pl.BlockSpec(x, lambda i, m, r=len(x): (0,) * r) for x, t in made],
        ),
        out_shape=[jax.ShapeDtypeStruct(x, t) for x, t in made],
        name="early_pass",
        compiler_params=pltpu.CompilerParams(vmem_limit_bytes=58 * 1024 * 1024),
    )(meta, *pieces, gain, *w_head)


def head_kernel(*refs):
    meta, pieces = refs[0], refs[1:9]
    (
        q_i, k_i, v_i, info_i, mine_i, do, gain, wq, wk, wv,
        normed, mine, part,
        q_s, do_s, k_s, v_s, dk_s, dv_s, e_s, p_s, docs, inv,
    ) = refs[9:]
    step = pl.program_id(0)
    half = meta[NBLK + 1]

    @pl.when(step == 0)
    def _():
        def put(p, carry):
            inv[meta[p]] = p
            return carry

        lax.fori_loop(0, NBLK, put, 0)
        docs[...] = jnp.zeros(docs.shape, F32)
        dk_s[...] = jnp.zeros(dk_s.shape, F32)
        dv_s[...] = jnp.zeros(dv_s.shape, F32)
        mine[...] = mine_i[...]
        for n in range(10):
            b = block_at(meta, n, EARLY)
            q_s[b] = q_i[n]
            k_s[b] = k_i[n]
            v_s[b] = v_i[n]
            docs[b // 4] += info_i[n]
        raw = []
        for c in range(2):
            down, up, first, second = pieces[c * 4 : c * 4 + 4]
            far = jnp.where(half == c, first[...], second[...])
            raw.append((down[0:BLOCK, :], down[BLOCK : BLOCK + EXTRA, 0:QROWS]))
            raw.append((up[0:BLOCK, :], up[BLOCK : BLOCK + EXTRA, 0:QROWS]))
            raw.append((far[0:BLOCK, :], far[BLOCK : BLOCK + EXTRA, 0:QROWS]))
        target = meta[half * 8 + meta[NBLK]]
        for n in range(0, 6, 2):
            rows = jnp.concatenate([raw[n][0], raw[n + 1][0]], axis=0)
            q, k, v = project(meta, n, rows, gain, wq, wk, wv, normed)
            for i in range(2):
                b = block_at(meta, n + i, LATE)
                q_s[b] = q[i]
                k_s[b] = k[i]
                v_s[b] = v[i]
                docs[b // 4] += raw[n + i][1].astype(F32)

                @pl.when(b == target)
                def _():
                    mine[...] = raw[n + i][0]

    q = q_s[pl.ds(step * 4, 4)].reshape(QROWS, HEAD)
    for t in range(4):
        do_s[t * HALF : (t + 1) * HALF, :] = do[place_of(inv[step * 4 + t])]
    info = docs[step]
    mine_docs = jnp.where(half == 0, info[0:1, :], info[1:2, :])
    lane = lax.broadcasted_iota(jnp.int32, (1, QROWS), 1)
    q_pos = step * KROWS + (lane // HALF) * BLOCK + half * HALF + lane % HALF
    known = docs[...]
    real = lax.broadcasted_iota(jnp.int32, known.shape, 1) < 2
    first = jnp.zeros((1, QROWS), F32)
    for number in range(1, 6):
        below = jnp.sum(jnp.where((known < number) & real, 1.0, 0.0))
        first = first + jnp.where(mine_docs == number, below, 0.0)
    q_first = first.astype(jnp.int32)
    low_tile = jnp.min(q_first) // KROWS

    def scores(g, total):
        s = dot(k_s[pl.ds(g * 4, 4)].reshape(KROWS, HEAD), q, 1, 1) * FACTOR
        j = g * KROWS + lax.broadcasted_iota(jnp.int32, (KROWS, QROWS), 0)
        e = jnp.where((j >= q_first) & (j <= q_pos), jnp.exp(s), 0.0)
        e_s[g] = e
        return total + jnp.sum(e, axis=0, keepdims=True)

    total = lax.fori_loop(low_tile, step + 1, scores, jnp.zeros((1, QROWS), F32))
    scale = 1.0 / total

    def deltas(g, delta):
        grad = dot(v_s[pl.ds(g * 4, 4)].reshape(KROWS, HEAD), do_s[...], 1, 1)
        p_s[g] = grad
        low = (e_s[g] * scale).astype(BF16)
        dv_s[g] += dot(low, do_s[...], 1, 0)
        return delta + jnp.sum(low.astype(F32) * grad, axis=0, keepdims=True)

    delta = lax.fori_loop(low_tile, step + 1, deltas, jnp.zeros((1, QROWS), F32))

    def grads(g, dq):
        ds = (e_s[g] * scale * (p_s[g] - delta)).astype(BF16)
        dk_s[g] += dot(ds, q, 1, 0)
        return dq + dot(ds, k_s[pl.ds(g * 4, 4)].reshape(KROWS, HEAD), 0, 0)

    dq = lax.fori_loop(low_tile, step + 1, grads, jnp.zeros((QROWS, HEAD), F32))
    dq = (dq * FACTOR).astype(BF16)
    part[pl.ds(step * 4, 4), 0:HALF, :] = dq.reshape(4, HALF, HEAD)

    @pl.when(step == STEPS - 1)
    def _():
        part[:, HALF : HALF + BLOCK, :] = (dk_s[...] * FACTOR).astype(BF16).reshape(NBLK, BLOCK, HEAD)
        part[:, HALF + BLOCK :, :] = dv_s[...].astype(BF16).reshape(NBLK, BLOCK, HEAD)


def head_pass(meta, pieces, made, do, gain, w_head):
    pack = (NBLK, HALF + 2 * BLOCK, HEAD)
    given = [*pieces, *made, do, gain, *w_head]
    outs = [(6, BLOCK, D), (BLOCK, D), pack]
    return pl.pallas_call(
        head_kernel,
        grid_spec=pltpu.PrefetchScalarGridSpec(
            num_scalar_prefetch=1,
            grid=(STEPS,),
            in_specs=[pl.BlockSpec(x.shape, lambda i, m, r=x.ndim: (0,) * r) for x in given],
            out_specs=[pl.BlockSpec(x, lambda i, m, r=len(x): (0,) * r) for x in outs],
            scratch_shapes=[
                pltpu.VMEM((NBLK, HALF, HEAD), BF16),
                pltpu.VMEM((QROWS, HEAD), BF16),
                pltpu.VMEM((NBLK, BLOCK, HEAD), BF16),
                pltpu.VMEM((NBLK, BLOCK, HEAD), BF16),
                pltpu.VMEM((STEPS, KROWS, HEAD), F32),
                pltpu.VMEM((STEPS, KROWS, HEAD), F32),
                pltpu.VMEM((STEPS, KROWS, QROWS), F32),
                pltpu.VMEM((STEPS, KROWS, QROWS), F32),
                pltpu.VMEM((STEPS, EXTRA, QROWS), F32),
                pltpu.SMEM((NBLK,), jnp.int32),
            ],
        ),
        out_shape=[jax.ShapeDtypeStruct(x, BF16) for x in outs],
        name="head_pass",
        compiler_params=pltpu.CompilerParams(vmem_limit_bytes=58 * 1024 * 1024),
    )(meta, *given)


def total_of(part, came, half, blocks):
    low = part[blocks, 0:HALF, :]
    high = came[blocks, 0:HALF, :]
    first = jnp.where(half == 0, low, high)
    second = jnp.where(half == 0, high, low)
    both = part[blocks, HALF:, :].astype(F32) + came[blocks, HALF:, :].astype(F32)
    return first, second, both.astype(BF16)


def weight_kernel(meta, n_early, n_late, part, came, here, there, grads):
    half = meta[NBLK + 1]
    y = meta[NBLK + 2]
    for n in range(NBLK):
        b = block_at(meta, n, EARLY) if n < 10 else block_at(meta, n - 10, LATE)
        first, second, both = total_of(part, came, half, b)
        grads[n, 0:HALF, 0:HEAD] = first
        grads[n, HALF:BLOCK, 0:HEAD] = second
        grads[n, :, HEAD : 2 * HEAD] = both[0:BLOCK]
        grads[n, :, 2 * HEAD :] = both[BLOCK:]
    made = dot(n_early[...].reshape(10 * BLOCK, D // 2), grads[0:10].reshape(10 * BLOCK, 3 * HEAD), 0, 0)
    made = made + dot(n_late[...].reshape(6 * BLOCK, D // 2), grads[10:16].reshape(6 * BLOCK, 3 * HEAD), 0, 0)
    every = made.reshape(8, 2, 32, 3 * HEAD)
    here[...] = jnp.where(y == 0, every[:, 0], every[:, 1]).astype(BF16)
    there[...] = jnp.where(y == 0, every[:, 1], every[:, 0]).astype(BF16)


def weight_pass(meta, n_early, n_late, part, came):
    pack = (NBLK, HALF + 2 * BLOCK, HEAD)
    shape = (8, 32, 3 * HEAD)
    grid_spec = pltpu.PrefetchScalarGridSpec(
        num_scalar_prefetch=1,
        grid=(1,),
        in_specs=[
            pl.BlockSpec((10, BLOCK, D // 2), lambda i, m: (0, 0, m[NBLK + 1])),
            pl.BlockSpec((6, BLOCK, D // 2), lambda i, m: (0, 0, m[NBLK + 1])),
            pl.BlockSpec(pack, lambda i, m: (0, 0, 0)),
            pl.BlockSpec(pack, lambda i, m: (0, 0, 0)),
        ],
        out_specs=[pl.BlockSpec(shape, lambda i, m: (0, 0, 0))] * 2,
        scratch_shapes=[pltpu.VMEM((NBLK, BLOCK, 3 * HEAD), BF16)],
    )
    return pl.pallas_call(
        weight_kernel,
        grid_spec=grid_spec,
        out_shape=[jax.ShapeDtypeStruct(shape, BF16)] * 2,
        name="weight_pass",
        compiler_params=pltpu.CompilerParams(vmem_limit_bytes=18 * 1024 * 1024),
    )(meta, n_early, n_late, part, came)


def join_kernel(meta, part, came, out):
    half = meta[NBLK + 1]
    for n in range(8):
        first, second, both = total_of(part, came, half, meta[half * 8 + n])
        out[n, 0:HALF, :] = first
        out[n, HALF:BLOCK, :] = second
        out[n, BLOCK:, :] = both


def join_pass(meta, part, came):
    shape = (NBLK, HALF + 2 * BLOCK, HEAD)
    made = (8, 3 * BLOCK, HEAD)
    grid_spec = pltpu.PrefetchScalarGridSpec(
        num_scalar_prefetch=1,
        grid=(1,),
        in_specs=[pl.BlockSpec(shape, lambda i, m: (0, 0, 0))] * 2,
        out_specs=pl.BlockSpec(made, lambda i, m: (0, 0, 0)),
    )
    return pl.pallas_call(
        join_kernel, grid_spec=grid_spec, out_shape=jax.ShapeDtypeStruct(made, BF16), name="join_pass", compiler_params=pltpu.CompilerParams(vmem_limit_bytes=10 * 1024 * 1024)
    )(meta, part, came)


def rows_kernel(back, mine, gain, w, out, grad, d_norm):
    step = pl.program_id(0)

    @pl.when(step == 0)
    def _():
        for h in range(HEADS):
            for n in range(3):
                to = n * D + h * HEAD
                grad[:, to : to + HEAD] = back[h, n * BLOCK : (n + 1) * BLOCK, :]

    d_norm[pl.ds(pl.multiple_of(step * 256, 256), 256), :] = dot(w[...], grad[...], 1, 1)

    @pl.when(step == STEPS - 1)
    def _():
        values = mine[...].astype(F32)
        inverse = lax.rsqrt(jnp.mean(values * values, axis=-1, keepdims=True) + EPS)
        unit = values * inverse
        gained = d_norm[...].T * gain[0:1, :]
        shared = jnp.mean(gained * unit, axis=-1, keepdims=True)
        out[...] = (inverse * (gained - unit * shared)).astype(BF16)


def rows_pass(back, mine, gain, w_qkv):
    return pl.pallas_call(
        rows_kernel,
        grid=(STEPS,),
        in_specs=[
            pl.BlockSpec((HEADS, 3 * BLOCK, HEAD), lambda i: (0, 0, 0)),
            pl.BlockSpec((BLOCK, D), lambda i: (0, 0)),
            pl.BlockSpec((8, D), lambda i: (0, 0)),
            pl.BlockSpec((D // STEPS, 3 * D), lambda i: (i, 0)),
        ],
        out_specs=pl.BlockSpec((BLOCK, D), lambda i: (0, 0)),
        scratch_shapes=[
            pltpu.VMEM((BLOCK, 3 * D), BF16),
            pltpu.VMEM((D, BLOCK), F32),
        ],
        out_shape=jax.ShapeDtypeStruct((BLOCK, D), BF16),
        name="rows_pass", compiler_params=pltpu.CompilerParams(vmem_limit_bytes=12 * 1024 * 1024),
    )(back, mine, gain, w_qkv)


def final_kernel(meta, own, other, out):
    half = meta[NBLK + 1]
    for side, ref in ((half, own), (1 - half, other)):
        row = pl.multiple_of(side * 32, 32)
        for h in range(HEADS):
            for n in range(3):
                value = ref[h, :, n * HEAD : (n + 1) * HEAD].astype(F32)
                out[pl.ds(row, 32), n * D + h * HEAD : n * D + (h + 1) * HEAD] = value * (1.0 / math.sqrt(32768))


def final_pass(meta, own, other):
    shape = (HEADS, 32, 3 * HEAD)
    grid_spec = pltpu.PrefetchScalarGridSpec(
        num_scalar_prefetch=1,
        grid=(1,),
        in_specs=[pl.BlockSpec(shape, lambda i, m: (0, 0, 0))] * 2,
        out_specs=pl.BlockSpec((64, 3 * D), lambda i, m: (0, 0)),
    )
    return pl.pallas_call(
        final_kernel, grid_spec=grid_spec, out_shape=jax.ShapeDtypeStruct((64, 3 * D), F32), name="final_pass", compiler_params=pltpu.CompilerParams(vmem_limit_bytes=6 * 1024 * 1024)
    )(meta, own, other)


def flip(x, axis, bit, size):
    return lax.ppermute(x, axis, [(i, i ^ bit) for i in range(size)])


def ring(x, axis, by, size):
    return lax.ppermute(x, axis, [(i, (i + by) % size) for i in range(size)])


def turn(x, by=0, other=0):
    pairs = []
    for y in range(2):
        for z in range(8):
            for c in range(2):
                pairs.append(((y * 8 + z) * 2 + c, (c * 8 + (z + by) % 8) * 2 + (y ^ other)))
    return lax.ppermute(x, ("y_lo", "z", "core"), pairs)


def added(a, b):
    return (a.astype(F32) + b.astype(F32)).astype(BF16)


def relay(payload):
    home = turn(payload)
    down, up = turn(payload, -1), turn(payload, 1)
    made = [home, down, up]
    for _ in range(2):
        down, up = ring(down, "z", -1, 8), ring(up, "z", 1, 8)
        made += [down, up]
    made.append(lax.ppermute(up, ("z", "core"), [(2 * n, 2 * ((n + 1) % 8)) for n in range(8)]))
    made.append(lax.ppermute(down, ("z", "core"), [(2 * n + 1, 2 * ((n + 7) % 8) + 1) for n in range(8)]))
    return made


def work(layer_rows, doc_ids, packing, norm_gain, w_qkv, d_attn):
    z = lax.axis_index("z")
    y = lax.axis_index("y_lo")
    x = lax.axis_index("x")
    core = lax.axis_index("core")
    halves = doc_ids[0].astype(BF16).reshape(2, 1, HALF)
    at = (jnp.arange(4, dtype=jnp.int32) == z % 4).astype(BF16)[None, :, None]
    info = jnp.pad((halves * at).reshape(2, QROWS), ((0, EXTRA - 2), (0, D - QROWS)))
    payload = jnp.concatenate([layer_rows[0], info], axis=0)
    order = turn(packing[0])
    parts = d_attn[0].reshape(2, HALF, HEADS, HEAD).transpose(2, 0, 1, 3)
    parts = turn(parts.reshape(NBLK, HALF, HEAD))
    meta = jnp.concatenate([order, jnp.stack([z, core, y, x]).astype(jnp.int32)])
    gain = jnp.broadcast_to(norm_gain[None, :], (8, D))
    w_head = [lax.dynamic_slice_in_dim(w_qkv, n * D + z * HEAD, HEAD, 1) for n in range(3)]

    pieces = relay(payload)
    others = [flip(piece, "core", 1, 2) for piece in pieces[:7]]
    others.append(lax.ppermute(pieces[7], "core", [(0, 1)]))
    others.append(lax.ppermute(pieces[8], "core", [(1, 0)]))
    early, *made = early_pass(meta, pieces[:5] + others[:5], gain, w_head)
    do = lax.all_to_all(parts, ("z", "core"), 0, 0, tiled=True)
    late, mine, part = head_pass(meta, pieces[5:] + others[5:], made, do, gain, w_head)
    came = flip(part, "core", 1, 2)
    here, there = weight_pass(meta, early, late, part, came)
    back = join_pass(meta, part, came)
    back = lax.all_to_all(back, "z", 0, 0, tiled=True)

    here = turn(here)
    there = turn(there, 0, 1)
    w_sum = added(here, there)
    w_sum = added(w_sum, flip(w_sum, "x", 1, 4))
    w_sum = added(w_sum, flip(w_sum, "x", 2, 4))
    w_sum = added(w_sum, flip(w_sum, "y_hi", 1, 2))
    w_sum = lax.all_to_all(w_sum, "z", 0, 0, tiled=True)
    other = flip(w_sum, "core", 1, 2)
    w_grad = final_pass(meta, w_sum, other)

    d_rows = rows_pass(back, mine, gain, w_qkv)
    d_rows = turn(d_rows)
    return (d_rows[None], w_grad)


def solution(mesh):
    fine = Mesh(
        mesh.devices.reshape(2, 8, 4, 2, 2), ("y_lo", "z", "x", "y_hi", "core")
    )
    seq = ("y_lo", "z")
    dp = ("x", "y_hi", "core")
    return jax.shard_map(
        work,
        mesh=fine,
        in_specs=(
            P(dp, seq, None),
            P(dp, seq),
            P(dp, None),
            P(),
            P(),
            P(dp, seq, None),
        ),
        out_specs=(P(dp, seq, None), P(seq, None)),
        check_vma=False,
    )
```

```python
import math

import jax
import jax.numpy as jnp
from jax import lax
from jax.experimental import pallas as pl
from jax.experimental.pallas import tpu as pltpu
from jax.sharding import Mesh
from jax.sharding import PartitionSpec as P

HEADS = 8
HEAD = 128
BLOCK = 128
HALF = 64
NBLK = 16
D = 1024
STEPS = 4
QROWS = 256
KROWS = 512
EXTRA = 8
FACTOR = 1.0 / math.sqrt(HEAD)
EPS = 1e-05
F32 = jnp.float32
BF16 = jnp.bfloat16


def dot(a, b, ca, cb):
    return lax.dot_general(a, b, (((ca,), (cb,)), ((), ())), preferred_element_type=F32)


def place_of(p):
    return (p % 8) * 2 + p // 8


PIECES = 9


def head_kernel(*refs):
    meta, pieces, others, rest = refs[0], refs[1 : 1 + PIECES], refs[1 + PIECES : 1 + 2 * PIECES], refs[1 + 2 * PIECES :]
    (
        do, gain, wq, wk, wv,
        normed, mine, part,
        rows_s, q_s, do_s, k_s, v_s, dk_s, dv_s, e_s, p_s, docs, inv, sems,
    ) = rest
    step = pl.program_id(0)
    z = meta[NBLK]
    half = meta[NBLK + 1]

    @pl.when(step == 0)
    def _():
        copies = []
        for c, group in enumerate((pieces, others)):
            side = half if c == 0 else 1 - half
            for n, ref in enumerate(group[:7]):
                offset = (0, 1, 7, 2, 6, 3, 5)[n]
                target = rows_s.at[side * 8 + (z + offset) % 8]
                copies.append(pltpu.make_async_copy(ref, target, sems.at[c * PIECES + n]))
        for copy in copies:
            copy.start()

        for c, group in enumerate((pieces, others)):
            far = rows_s.at[(half if c == 0 else 1 - half) * 8 + (z + 4) % 8]
            for n in range(2):

                @pl.when(half == (n if c == 0 else 1 - n))
                def _():
                    copy = pltpu.make_async_copy(group[7 + n], far, sems.at[c * PIECES + 7 + n])
                    copy.start()
                    copy.wait()

        def put(p, carry):
            inv[meta[p]] = p
            return carry

        lax.fori_loop(0, NBLK, put, 0)
        docs[...] = jnp.full(docs.shape, 1000.0, F32)
        dk_s[...] = jnp.zeros(dk_s.shape, F32)
        dv_s[...] = jnp.zeros(dv_s.shape, F32)
        for copy in copies:
            copy.wait()
        mine[...] = rows_s[meta[half * 8 + z], 0:BLOCK, :]

    rows = rows_s[pl.ds(step * 4, 4), 0:BLOCK, :].astype(F32)
    inverse = lax.rsqrt(jnp.mean(rows * rows, axis=-1, keepdims=True) + EPS)
    nrm = (rows * inverse * gain[0:1, :][None]).astype(BF16)
    normed[...] = nrm
    nrm = nrm.reshape(KROWS, D)
    k_s[step] = dot(nrm, wk[...], 1, 0).astype(BF16)
    v_s[step] = dot(nrm, wv[...], 1, 0).astype(BF16)
    own = pl.multiple_of(half * HALF, HALF)
    qn = normed[:, pl.ds(own, HALF), :].reshape(QROWS, D)
    q_s[...] = dot(qn, wq[...], 1, 0).astype(BF16)
    for t in range(4):
        do_s[t * HALF : (t + 1) * HALF, :] = do[place_of(inv[step * 4 + t])]

    info = jnp.sum(rows_s[pl.ds(step * 4, 4), BLOCK : BLOCK + EXTRA, 0:QROWS].astype(F32), axis=0)
    docs[step] = info
    mine_docs = jnp.where(half == 0, info[0:1, :], info[1:2, :])
    lane = lax.broadcasted_iota(jnp.int32, (1, QROWS), 1)
    q_pos = step * KROWS + (lane // HALF) * BLOCK + half * HALF + lane % HALF
    known = docs[...]
    real = lax.broadcasted_iota(jnp.int32, known.shape, 1) < 2
    first = jnp.zeros((1, QROWS), F32)
    for number in range(1, 6):
        below = jnp.sum(jnp.where((known < number) & real, 1.0, 0.0))
        first = first + jnp.where(mine_docs == number, below, 0.0)
    q_first = first.astype(jnp.int32)
    low_tile = jnp.min(q_first) // KROWS

    def scores(g, total):
        s = dot(k_s[g], q_s[...], 1, 1) * FACTOR
        j = g * KROWS + lax.broadcasted_iota(jnp.int32, (KROWS, QROWS), 0)
        e = jnp.where((j >= q_first) & (j <= q_pos), jnp.exp(s), 0.0)
        e_s[g] = e
        return total + jnp.sum(e, axis=0, keepdims=True)

    total = lax.fori_loop(low_tile, step + 1, scores, jnp.zeros((1, QROWS), F32))
    scale = 1.0 / total

    def deltas(g, delta):
        grad = dot(v_s[g], do_s[...], 1, 1)
        p_s[g] = grad
        low = (e_s[g] * scale).astype(BF16)
        dv_s[g] += dot(low, do_s[...], 1, 0)
        return delta + jnp.sum(low.astype(F32) * grad, axis=0, keepdims=True)

    delta = lax.fori_loop(low_tile, step + 1, deltas, jnp.zeros((1, QROWS), F32))

    def grads(g, dq):
        ds = (e_s[g] * scale * (p_s[g] - delta)).astype(BF16)
        dk_s[g] += dot(ds, q_s[...], 1, 0)
        return dq + dot(ds, k_s[g], 0, 0)

    dq = lax.fori_loop(low_tile, step + 1, grads, jnp.zeros((QROWS, HEAD), F32))
    dq = (dq * FACTOR).astype(BF16)
    part[pl.ds(step * 4, 4), 0:HALF, :] = dq.reshape(4, HALF, HEAD)

    @pl.when(step == STEPS - 1)
    def _():
        part[:, HALF : HALF + BLOCK, :] = (dk_s[...] * FACTOR).astype(BF16).reshape(NBLK, BLOCK, HEAD)
        part[:, HALF + BLOCK :, :] = dv_s[...].astype(BF16).reshape(NBLK, BLOCK, HEAD)


def head_pass(meta, pieces, others, do, gain, w_head):
    pack = (NBLK, HALF + 2 * BLOCK, HEAD)
    grid_spec = pltpu.PrefetchScalarGridSpec(
        num_scalar_prefetch=1,
        grid=(STEPS,),
        in_specs=[pl.BlockSpec(memory_space=pl.ANY)] * (2 * PIECES)
        + [
            pl.BlockSpec((NBLK, HALF, HEAD), lambda i, m: (0, 0, 0)),
            pl.BlockSpec((8, D), lambda i, m: (0, 0)),
        ]
        + [pl.BlockSpec((D, HEAD), lambda i, m: (0, 0))] * 3,
        out_specs=[
            pl.BlockSpec((4, BLOCK, D), lambda i, m: (i, 0, 0)),
            pl.BlockSpec((BLOCK, D), lambda i, m: (0, 0)),
            pl.BlockSpec(pack, lambda i, m: (0, 0, 0)),
        ],
        scratch_shapes=[
            pltpu.VMEM((NBLK, BLOCK + EXTRA, D), BF16),
            pltpu.VMEM((QROWS, HEAD), BF16),
            pltpu.VMEM((QROWS, HEAD), BF16),
            pltpu.VMEM((STEPS, KROWS, HEAD), BF16),
            pltpu.VMEM((STEPS, KROWS, HEAD), BF16),
            pltpu.VMEM((STEPS, KROWS, HEAD), F32),
            pltpu.VMEM((STEPS, KROWS, HEAD), F32),
            pltpu.VMEM((STEPS, KROWS, QROWS), F32),
            pltpu.VMEM((STEPS, KROWS, QROWS), F32),
            pltpu.VMEM((STEPS, EXTRA, QROWS), F32),
            pltpu.SMEM((NBLK,), jnp.int32),
            pltpu.SemaphoreType.DMA((2 * PIECES,)),
        ],
    )
    return pl.pallas_call(
        head_kernel,
        grid_spec=grid_spec,
        out_shape=[
            jax.ShapeDtypeStruct((NBLK, BLOCK, D), BF16),
            jax.ShapeDtypeStruct((BLOCK, D), BF16),
            jax.ShapeDtypeStruct(pack, BF16),
        ],
        name="head_pass", compiler_params=pltpu.CompilerParams(vmem_limit_bytes=26 * 1024 * 1024),
    )(meta, *pieces, *others, do, gain, *w_head)


def total_of(part, came, half, blocks):
    low = part[blocks, 0:HALF, :]
    high = came[blocks, 0:HALF, :]
    first = jnp.where(half == 0, low, high)
    second = jnp.where(half == 0, high, low)
    both = part[blocks, HALF:, :].astype(F32) + came[blocks, HALF:, :].astype(F32)
    return first, second, both.astype(BF16)


def weight_kernel(meta, normed, part, came, here, there, dw_s):
    step = pl.program_id(0)
    half = meta[NBLK + 1]
    y = meta[NBLK + 2]
    first, second, both = total_of(part, came, half, slice(None))
    dq = jnp.concatenate([first, second], axis=1).reshape(KROWS, HEAD)
    dk = both[:, 0:BLOCK, :].reshape(KROWS, HEAD)
    dv = both[:, BLOCK:, :].reshape(KROWS, HEAD)
    grads = jnp.concatenate([dq, dk, dv], axis=1)
    made = dot(normed[...].reshape(KROWS, D // 2), grads, 0, 0)

    @pl.when(step == 0)
    def _():
        dw_s[...] = made

    @pl.when(step > 0)
    def _():
        dw_s[...] += made

    @pl.when(step == STEPS - 1)
    def _():
        every = dw_s[...].reshape(8, 2, 32, 3 * HEAD)
        here[...] = jnp.where(y == 0, every[:, 0], every[:, 1]).astype(BF16)
        there[...] = jnp.where(y == 0, every[:, 1], every[:, 0]).astype(BF16)


def weight_pass(meta, normed, part, came):
    pack = (4, HALF + 2 * BLOCK, HEAD)
    shape = (8, 32, 3 * HEAD)
    grid_spec = pltpu.PrefetchScalarGridSpec(
        num_scalar_prefetch=1,
        grid=(STEPS,),
        in_specs=[
            pl.BlockSpec((4, BLOCK, D // 2), lambda i, m: (i, 0, m[NBLK + 1])),
            pl.BlockSpec(pack, lambda i, m: (i, 0, 0)),
            pl.BlockSpec(pack, lambda i, m: (i, 0, 0)),
        ],
        out_specs=[pl.BlockSpec(shape, lambda i, m: (0, 0, 0))] * 2,
        scratch_shapes=[pltpu.VMEM((D // 2, 3 * HEAD), F32)],
    )
    return pl.pallas_call(
        weight_kernel,
        grid_spec=grid_spec,
        out_shape=[jax.ShapeDtypeStruct(shape, BF16)] * 2,
        name="weight_pass", compiler_params=pltpu.CompilerParams(vmem_limit_bytes=10 * 1024 * 1024),
    )(meta, normed, part, came)


def join_kernel(meta, part, came, out):
    half = meta[NBLK + 1]
    for n in range(8):
        first, second, both = total_of(part, came, half, meta[half * 8 + n])
        out[n, 0:HALF, :] = first
        out[n, HALF:BLOCK, :] = second
        out[n, BLOCK:, :] = both


def join_pass(meta, part, came):
    shape = (NBLK, HALF + 2 * BLOCK, HEAD)
    made = (8, 3 * BLOCK, HEAD)
    grid_spec = pltpu.PrefetchScalarGridSpec(
        num_scalar_prefetch=1,
        grid=(1,),
        in_specs=[pl.BlockSpec(shape, lambda i, m: (0, 0, 0))] * 2,
        out_specs=pl.BlockSpec(made, lambda i, m: (0, 0, 0)),
    )
    return pl.pallas_call(
        join_kernel, grid_spec=grid_spec, out_shape=jax.ShapeDtypeStruct(made, BF16), name="join_pass", compiler_params=pltpu.CompilerParams(vmem_limit_bytes=10 * 1024 * 1024)
    )(meta, part, came)


def rows_kernel(back, mine, gain, w, out, grad, d_norm):
    step = pl.program_id(0)

    @pl.when(step == 0)
    def _():
        for h in range(HEADS):
            for n in range(3):
                to = n * D + h * HEAD
                grad[:, to : to + HEAD] = back[h, n * BLOCK : (n + 1) * BLOCK, :]

    d_norm[pl.ds(pl.multiple_of(step * 256, 256), 256), :] = dot(w[...], grad[...], 1, 1)

    @pl.when(step == STEPS - 1)
    def _():
        values = mine[...].astype(F32)
        inverse = lax.rsqrt(jnp.mean(values * values, axis=-1, keepdims=True) + EPS)
        unit = values * inverse
        gained = d_norm[...].T * gain[0:1, :]
        shared = jnp.mean(gained * unit, axis=-1, keepdims=True)
        out[...] = (inverse * (gained - unit * shared)).astype(BF16)


def rows_pass(back, mine, gain, w_qkv):
    return pl.pallas_call(
        rows_kernel,
        grid=(STEPS,),
        in_specs=[
            pl.BlockSpec((HEADS, 3 * BLOCK, HEAD), lambda i: (0, 0, 0)),
            pl.BlockSpec((BLOCK, D), lambda i: (0, 0)),
            pl.BlockSpec((8, D), lambda i: (0, 0)),
            pl.BlockSpec((D // STEPS, 3 * D), lambda i: (i, 0)),
        ],
        out_specs=pl.BlockSpec((BLOCK, D), lambda i: (0, 0)),
        scratch_shapes=[
            pltpu.VMEM((BLOCK, 3 * D), BF16),
            pltpu.VMEM((D, BLOCK), F32),
        ],
        out_shape=jax.ShapeDtypeStruct((BLOCK, D), BF16),
        name="rows_pass", compiler_params=pltpu.CompilerParams(vmem_limit_bytes=12 * 1024 * 1024),
    )(back, mine, gain, w_qkv)


def final_kernel(meta, own, other, out):
    half = meta[NBLK + 1]
    for side, ref in ((half, own), (1 - half, other)):
        row = pl.multiple_of(side * 32, 32)
        for h in range(HEADS):
            for n in range(3):
                value = ref[h, :, n * HEAD : (n + 1) * HEAD].astype(F32)
                out[pl.ds(row, 32), n * D + h * HEAD : n * D + (h + 1) * HEAD] = value * (1.0 / math.sqrt(32768))


def final_pass(meta, own, other):
    shape = (HEADS, 32, 3 * HEAD)
    grid_spec = pltpu.PrefetchScalarGridSpec(
        num_scalar_prefetch=1,
        grid=(1,),
        in_specs=[pl.BlockSpec(shape, lambda i, m: (0, 0, 0))] * 2,
        out_specs=pl.BlockSpec((64, 3 * D), lambda i, m: (0, 0)),
    )
    return pl.pallas_call(
        final_kernel, grid_spec=grid_spec, out_shape=jax.ShapeDtypeStruct((64, 3 * D), F32), name="final_pass", compiler_params=pltpu.CompilerParams(vmem_limit_bytes=6 * 1024 * 1024)
    )(meta, own, other)


def flip(x, axis, bit, size):
    return lax.ppermute(x, axis, [(i, i ^ bit) for i in range(size)])


def ring(x, axis, by, size):
    return lax.ppermute(x, axis, [(i, (i + by) % size) for i in range(size)])


def turn(x, by=0, other=0):
    pairs = []
    for y in range(2):
        for z in range(8):
            for c in range(2):
                pairs.append(((y * 8 + z) * 2 + c, (c * 8 + (z + by) % 8) * 2 + (y ^ other)))
    return lax.ppermute(x, ("y_lo", "z", "core"), pairs)


def added(a, b):
    return (a.astype(F32) + b.astype(F32)).astype(BF16)


def relay(payload):
    home = turn(payload)
    down, up = turn(payload, -1), turn(payload, 1)
    made = [home, down, up]
    for _ in range(2):
        down, up = ring(down, "z", -1, 8), ring(up, "z", 1, 8)
        made += [down, up]
    made.append(lax.ppermute(up, ("z", "core"), [(2 * n, 2 * ((n + 1) % 8)) for n in range(8)]))
    made.append(lax.ppermute(down, ("z", "core"), [(2 * n + 1, 2 * ((n + 7) % 8) + 1) for n in range(8)]))
    return made


def work(layer_rows, doc_ids, packing, norm_gain, w_qkv, d_attn):
    z = lax.axis_index("z")
    y = lax.axis_index("y_lo")
    x = lax.axis_index("x")
    core = lax.axis_index("core")
    halves = doc_ids[0].astype(BF16).reshape(2, 1, HALF)
    at = (jnp.arange(4, dtype=jnp.int32) == z % 4).astype(BF16)[None, :, None]
    info = jnp.pad((halves * at).reshape(2, QROWS), ((0, EXTRA - 2), (0, D - QROWS)))
    payload = jnp.concatenate([layer_rows[0], info], axis=0)
    order = turn(packing[0])
    parts = d_attn[0].reshape(2, HALF, HEADS, HEAD).transpose(2, 0, 1, 3)
    parts = turn(parts.reshape(NBLK, HALF, HEAD))
    meta = jnp.concatenate([order, jnp.stack([z, core, y, x]).astype(jnp.int32)])
    gain = jnp.broadcast_to(norm_gain[None, :], (8, D))
    w_head = [lax.dynamic_slice_in_dim(w_qkv, n * D + z * HEAD, HEAD, 1) for n in range(3)]

    pieces = relay(payload)
    others = [flip(piece, "core", 1, 2) for piece in pieces[:7]]
    others.append(lax.ppermute(pieces[7], "core", [(0, 1)]))
    others.append(lax.ppermute(pieces[8], "core", [(1, 0)]))
    do = lax.all_to_all(parts, ("z", "core"), 0, 0, tiled=True)
    normed, mine, part = head_pass(meta, pieces, others, do, gain, w_head)
    came = flip(part, "core", 1, 2)
    here, there = weight_pass(meta, normed, part, came)
    back = join_pass(meta, part, came)
    back = lax.all_to_all(back, "z", 0, 0, tiled=True)

    here = turn(here)
    there = turn(there, 0, 1)
    w_sum = added(here, there)
    w_sum = added(w_sum, flip(w_sum, "x", 1, 4))
    w_sum = added(w_sum, flip(w_sum, "x", 2, 4))
    w_sum = added(w_sum, flip(w_sum, "y_hi", 1, 2))
    w_sum = lax.all_to_all(w_sum, "z", 0, 0, tiled=True)
    other = flip(w_sum, "core", 1, 2)
    w_grad = final_pass(meta, w_sum, other)

    d_rows = rows_pass(back, mine, gain, w_qkv)
    d_rows = turn(d_rows)
    return (d_rows[None], w_grad)


def solution(mesh):
    fine = Mesh(
        mesh.devices.reshape(2, 8, 4, 2, 2), ("y_lo", "z", "x", "y_hi", "core")
    )
    seq = ("y_lo", "z")
    dp = ("x", "y_hi", "core")
    return jax.shard_map(
        work,
        mesh=fine,
        in_specs=(
            P(dp, seq, None),
            P(dp, seq),
            P(dp, None),
            P(),
            P(),
            P(dp, seq, None),
        ),
        out_specs=(P(dp, seq, None), P(seq, None)),
        check_vma=False,
    )
```

```python
import math

import jax
import jax.numpy as jnp
from jax import lax
from jax.experimental import pallas as pl
from jax.experimental.pallas import tpu as pltpu
from jax.sharding import Mesh
from jax.sharding import PartitionSpec as P

HEADS = 8
HEAD = 128
BLOCK = 128
HALF = 64
NBLK = 16
D = 1024
STEPS = 4
QROWS = 256
KROWS = 512
EXTRA = 8
FACTOR = 1.0 / math.sqrt(HEAD)
EPS = 1e-05
F32 = jnp.float32
BF16 = jnp.bfloat16


def dot(a, b, ca, cb):
    return lax.dot_general(a, b, (((ca,), (cb,)), ((), ())), preferred_element_type=F32)


def place_of(p):
    return (p % 8) * 2 + p // 8


PIECES = 9


def head_kernel(*refs):
    meta, pieces, others, rest = refs[0], refs[1 : 1 + PIECES], refs[1 + PIECES : 1 + 2 * PIECES], refs[1 + 2 * PIECES :]
    (
        do, gain, wq, wk, wv,
        normed, mine, part,
        rows_s, q_s, do_s, k_s, v_s, dk_s, dv_s, e_s, p_s, docs, inv, sems,
    ) = rest
    step = pl.program_id(0)
    z = meta[NBLK]
    half = meta[NBLK + 1]

    @pl.when(step == 0)
    def _():
        copies = []
        for c, group in enumerate((pieces, others)):
            side = half if c == 0 else 1 - half
            for n, ref in enumerate(group):
                offset = (0, 1, 7, 2, 6, 3, 5, 4, 4)[n]
                target = rows_s.at[side * 8 + (z + offset) % 8]
                if n == 7:
                    target = target.at[0:HALF]
                elif n == 8:
                    target = target.at[HALF : BLOCK + EXTRA]
                copies.append(pltpu.make_async_copy(ref, target, sems.at[c * PIECES + n]))
        for copy in copies:
            copy.start()

        def put(p, carry):
            inv[meta[p]] = p
            return carry

        lax.fori_loop(0, NBLK, put, 0)
        docs[...] = jnp.full(docs.shape, 1000.0, F32)
        dk_s[...] = jnp.zeros(dk_s.shape, F32)
        dv_s[...] = jnp.zeros(dv_s.shape, F32)
        for copy in copies:
            copy.wait()
        mine[...] = rows_s[meta[half * 8 + z], 0:BLOCK, :]

    rows = rows_s[pl.ds(step * 4, 4), 0:BLOCK, :].astype(F32)
    inverse = lax.rsqrt(jnp.mean(rows * rows, axis=-1, keepdims=True) + EPS)
    nrm = (rows * inverse * gain[0:1, :][None]).astype(BF16)
    normed[...] = nrm
    nrm = nrm.reshape(KROWS, D)
    k_s[step] = dot(nrm, wk[...], 1, 0).astype(BF16)
    v_s[step] = dot(nrm, wv[...], 1, 0).astype(BF16)
    own = pl.multiple_of(half * HALF, HALF)
    qn = normed[:, pl.ds(own, HALF), :].reshape(QROWS, D)
    q_s[...] = dot(qn, wq[...], 1, 0).astype(BF16)
    for t in range(4):
        do_s[t * HALF : (t + 1) * HALF, :] = do[place_of(inv[step * 4 + t])]

    info = jnp.sum(rows_s[pl.ds(step * 4, 4), BLOCK : BLOCK + EXTRA, 0:QROWS].astype(F32), axis=0)
    docs[step] = info
    mine_docs = jnp.where(half == 0, info[0:1, :], info[1:2, :])
    lane = lax.broadcasted_iota(jnp.int32, (1, QROWS), 1)
    q_pos = step * KROWS + (lane // HALF) * BLOCK + half * HALF + lane % HALF
    known = docs[...]
    real = lax.broadcasted_iota(jnp.int32, known.shape, 1) < 2
    first = jnp.zeros((1, QROWS), F32)
    for number in range(1, 6):
        below = jnp.sum(jnp.where((known < number) & real, 1.0, 0.0))
        first = first + jnp.where(mine_docs == number, below, 0.0)
    q_first = first.astype(jnp.int32)
    low_tile = jnp.min(q_first) // KROWS

    def scores(g, total):
        s = dot(k_s[g], q_s[...], 1, 1) * FACTOR
        j = g * KROWS + lax.broadcasted_iota(jnp.int32, (KROWS, QROWS), 0)
        e = jnp.where((j >= q_first) & (j <= q_pos), jnp.exp(s), 0.0)
        e_s[g] = e
        return total + jnp.sum(e, axis=0, keepdims=True)

    total = lax.fori_loop(low_tile, step + 1, scores, jnp.zeros((1, QROWS), F32))
    scale = 1.0 / total

    def deltas(g, delta):
        grad = dot(v_s[g], do_s[...], 1, 1)
        p_s[g] = grad
        low = (e_s[g] * scale).astype(BF16)
        dv_s[g] += dot(low, do_s[...], 1, 0)
        return delta + jnp.sum(low.astype(F32) * grad, axis=0, keepdims=True)

    delta = lax.fori_loop(low_tile, step + 1, deltas, jnp.zeros((1, QROWS), F32))

    def grads(g, dq):
        ds = (e_s[g] * scale * (p_s[g] - delta)).astype(BF16)
        dk_s[g] += dot(ds, q_s[...], 1, 0)
        return dq + dot(ds, k_s[g], 0, 0)

    dq = lax.fori_loop(low_tile, step + 1, grads, jnp.zeros((QROWS, HEAD), F32))
    dq = (dq * FACTOR).astype(BF16)
    part[pl.ds(step * 4, 4), 0:HALF, :] = dq.reshape(4, HALF, HEAD)

    @pl.when(step == STEPS - 1)
    def _():
        part[:, HALF : HALF + BLOCK, :] = (dk_s[...] * FACTOR).astype(BF16).reshape(NBLK, BLOCK, HEAD)
        part[:, HALF + BLOCK :, :] = dv_s[...].astype(BF16).reshape(NBLK, BLOCK, HEAD)


def head_pass(meta, pieces, others, do, gain, w_head):
    pack = (NBLK, HALF + 2 * BLOCK, HEAD)
    grid_spec = pltpu.PrefetchScalarGridSpec(
        num_scalar_prefetch=1,
        grid=(STEPS,),
        in_specs=[pl.BlockSpec(memory_space=pl.ANY)] * (2 * PIECES)
        + [
            pl.BlockSpec((NBLK, HALF, HEAD), lambda i, m: (0, 0, 0)),
            pl.BlockSpec((8, D), lambda i, m: (0, 0)),
        ]
        + [pl.BlockSpec((D, HEAD), lambda i, m: (0, 0))] * 3,
        out_specs=[
            pl.BlockSpec((4, BLOCK, D), lambda i, m: (i, 0, 0)),
            pl.BlockSpec((BLOCK, D), lambda i, m: (0, 0)),
            pl.BlockSpec(pack, lambda i, m: (0, 0, 0)),
        ],
        scratch_shapes=[
            pltpu.VMEM((NBLK, BLOCK + EXTRA, D), BF16),
            pltpu.VMEM((QROWS, HEAD), BF16),
            pltpu.VMEM((QROWS, HEAD), BF16),
            pltpu.VMEM((STEPS, KROWS, HEAD), BF16),
            pltpu.VMEM((STEPS, KROWS, HEAD), BF16),
            pltpu.VMEM((STEPS, KROWS, HEAD), F32),
            pltpu.VMEM((STEPS, KROWS, HEAD), F32),
            pltpu.VMEM((STEPS, KROWS, QROWS), F32),
            pltpu.VMEM((STEPS, KROWS, QROWS), F32),
            pltpu.VMEM((STEPS, EXTRA, QROWS), F32),
            pltpu.SMEM((NBLK,), jnp.int32),
            pltpu.SemaphoreType.DMA((2 * PIECES,)),
        ],
    )
    return pl.pallas_call(
        head_kernel,
        grid_spec=grid_spec,
        out_shape=[
            jax.ShapeDtypeStruct((NBLK, BLOCK, D), BF16),
            jax.ShapeDtypeStruct((BLOCK, D), BF16),
            jax.ShapeDtypeStruct(pack, BF16),
        ],
        name="head_pass", compiler_params=pltpu.CompilerParams(vmem_limit_bytes=26 * 1024 * 1024),
    )(meta, *pieces, *others, do, gain, *w_head)


def total_of(part, came, half, blocks):
    low = part[blocks, 0:HALF, :]
    high = came[blocks, 0:HALF, :]
    first = jnp.where(half == 0, low, high)
    second = jnp.where(half == 0, high, low)
    both = part[blocks, HALF:, :].astype(F32) + came[blocks, HALF:, :].astype(F32)
    return first, second, both.astype(BF16)


def weight_kernel(meta, normed, part, came, here, there, grads):
    half = meta[NBLK + 1]
    y = meta[NBLK + 2]
    for b in range(NBLK):
        first, second, both = total_of(part, came, half, b)
        grads[b, 0:HALF, 0:HEAD] = first
        grads[b, HALF:BLOCK, 0:HEAD] = second
        grads[b, :, HEAD : 2 * HEAD] = both[0:BLOCK]
        grads[b, :, 2 * HEAD :] = both[BLOCK:]
    made = dot(normed[...].reshape(NBLK * BLOCK, D // 2), grads[...].reshape(NBLK * BLOCK, 3 * HEAD), 0, 0)
    every = made.reshape(8, 2, 32, 3 * HEAD)
    here[...] = jnp.where(y == 0, every[:, 0], every[:, 1]).astype(BF16)
    there[...] = jnp.where(y == 0, every[:, 1], every[:, 0]).astype(BF16)


def weight_pass(meta, normed, part, came):
    pack = (NBLK, HALF + 2 * BLOCK, HEAD)
    shape = (8, 32, 3 * HEAD)
    grid_spec = pltpu.PrefetchScalarGridSpec(
        num_scalar_prefetch=1,
        grid=(1,),
        in_specs=[
            pl.BlockSpec((NBLK, BLOCK, D // 2), lambda i, m: (0, 0, m[NBLK + 1])),
            pl.BlockSpec(pack, lambda i, m: (0, 0, 0)),
            pl.BlockSpec(pack, lambda i, m: (0, 0, 0)),
        ],
        out_specs=[pl.BlockSpec(shape, lambda i, m: (0, 0, 0))] * 2,
        scratch_shapes=[pltpu.VMEM((NBLK, BLOCK, 3 * HEAD), BF16)],
    )
    return pl.pallas_call(
        weight_kernel,
        grid_spec=grid_spec,
        out_shape=[jax.ShapeDtypeStruct(shape, BF16)] * 2,
        name="weight_pass",
        compiler_params=pltpu.CompilerParams(vmem_limit_bytes=18 * 1024 * 1024),
    )(meta, normed, part, came)


def join_kernel(meta, part, came, out):
    half = meta[NBLK + 1]
    for n in range(8):
        first, second, both = total_of(part, came, half, meta[half * 8 + n])
        out[n, 0:HALF, :] = first
        out[n, HALF:BLOCK, :] = second
        out[n, BLOCK:, :] = both


def join_pass(meta, part, came):
    shape = (NBLK, HALF + 2 * BLOCK, HEAD)
    made = (8, 3 * BLOCK, HEAD)
    grid_spec = pltpu.PrefetchScalarGridSpec(
        num_scalar_prefetch=1,
        grid=(1,),
        in_specs=[pl.BlockSpec(shape, lambda i, m: (0, 0, 0))] * 2,
        out_specs=pl.BlockSpec(made, lambda i, m: (0, 0, 0)),
    )
    return pl.pallas_call(
        join_kernel, grid_spec=grid_spec, out_shape=jax.ShapeDtypeStruct(made, BF16), name="join_pass", compiler_params=pltpu.CompilerParams(vmem_limit_bytes=10 * 1024 * 1024)
    )(meta, part, came)


def rows_kernel(back, mine, gain, w, out, grad, d_norm):
    step = pl.program_id(0)

    @pl.when(step == 0)
    def _():
        for h in range(HEADS):
            for n in range(3):
                to = n * D + h * HEAD
                grad[:, to : to + HEAD] = back[h, n * BLOCK : (n + 1) * BLOCK, :]

    d_norm[pl.ds(pl.multiple_of(step * 256, 256), 256), :] = dot(w[...], grad[...], 1, 1)

    @pl.when(step == STEPS - 1)
    def _():
        values = mine[...].astype(F32)
        inverse = lax.rsqrt(jnp.mean(values * values, axis=-1, keepdims=True) + EPS)
        unit = values * inverse
        gained = d_norm[...].T * gain[0:1, :]
        shared = jnp.mean(gained * unit, axis=-1, keepdims=True)
        out[...] = (inverse * (gained - unit * shared)).astype(BF16)


def rows_pass(back, mine, gain, w_qkv):
    return pl.pallas_call(
        rows_kernel,
        grid=(STEPS,),
        in_specs=[
            pl.BlockSpec((HEADS, 3 * BLOCK, HEAD), lambda i: (0, 0, 0)),
            pl.BlockSpec((BLOCK, D), lambda i: (0, 0)),
            pl.BlockSpec((8, D), lambda i: (0, 0)),
            pl.BlockSpec((D // STEPS, 3 * D), lambda i: (i, 0)),
        ],
        out_specs=pl.BlockSpec((BLOCK, D), lambda i: (0, 0)),
        scratch_shapes=[
            pltpu.VMEM((BLOCK, 3 * D), BF16),
            pltpu.VMEM((D, BLOCK), F32),
        ],
        out_shape=jax.ShapeDtypeStruct((BLOCK, D), BF16),
        name="rows_pass", compiler_params=pltpu.CompilerParams(vmem_limit_bytes=12 * 1024 * 1024),
    )(back, mine, gain, w_qkv)


def final_kernel(meta, own, other, out):
    half = meta[NBLK + 1]
    for side, ref in ((half, own), (1 - half, other)):
        row = pl.multiple_of(side * 32, 32)
        for h in range(HEADS):
            for n in range(3):
                value = ref[h, :, n * HEAD : (n + 1) * HEAD].astype(F32)
                out[pl.ds(row, 32), n * D + h * HEAD : n * D + (h + 1) * HEAD] = value * (1.0 / math.sqrt(32768))


def final_pass(meta, own, other):
    shape = (HEADS, 32, 3 * HEAD)
    grid_spec = pltpu.PrefetchScalarGridSpec(
        num_scalar_prefetch=1,
        grid=(1,),
        in_specs=[pl.BlockSpec(shape, lambda i, m: (0, 0, 0))] * 2,
        out_specs=pl.BlockSpec((64, 3 * D), lambda i, m: (0, 0)),
    )
    return pl.pallas_call(
        final_kernel, grid_spec=grid_spec, out_shape=jax.ShapeDtypeStruct((64, 3 * D), F32), name="final_pass", compiler_params=pltpu.CompilerParams(vmem_limit_bytes=6 * 1024 * 1024)
    )(meta, own, other)


def flip(x, axis, bit, size):
    return lax.ppermute(x, axis, [(i, i ^ bit) for i in range(size)])


def ring(x, axis, by, size):
    return lax.ppermute(x, axis, [(i, (i + by) % size) for i in range(size)])


def turn(x, by=0, other=0):
    pairs = []
    for y in range(2):
        for z in range(8):
            for c in range(2):
                pairs.append(((y * 8 + z) * 2 + c, (c * 8 + (z + by) % 8) * 2 + (y ^ other)))
    return lax.ppermute(x, ("y_lo", "z", "core"), pairs)


def added(a, b):
    return (a.astype(F32) + b.astype(F32)).astype(BF16)


def relay(payload):
    home = turn(payload)
    down, up = turn(payload, -1), turn(payload, 1)
    made = [home, down, up]
    for _ in range(2):
        down, up = ring(down, "z", -1, 8), ring(up, "z", 1, 8)
        made += [down, up]
    far = ring(up[:HALF], "z", 1, 8)
    made.append(far)
    far = ring(down[HALF:], "z", -1, 8)
    made.append(far)
    return made


def work(layer_rows, doc_ids, packing, norm_gain, w_qkv, d_attn):
    z = lax.axis_index("z")
    y = lax.axis_index("y_lo")
    x = lax.axis_index("x")
    core = lax.axis_index("core")
    halves = doc_ids[0].astype(BF16).reshape(2, 1, HALF)
    at = (jnp.arange(4, dtype=jnp.int32) == z % 4).astype(BF16)[None, :, None]
    info = jnp.pad((halves * at).reshape(2, QROWS), ((0, EXTRA - 2), (0, D - QROWS)))
    payload = jnp.concatenate([layer_rows[0], info], axis=0)
    order = turn(packing[0])
    parts = d_attn[0].reshape(2, HALF, HEADS, HEAD).transpose(2, 0, 1, 3)
    parts = turn(parts.reshape(NBLK, HALF, HEAD))
    meta = jnp.concatenate([order, jnp.stack([z, core, y, x]).astype(jnp.int32)])
    gain = jnp.broadcast_to(norm_gain[None, :], (8, D))
    w_head = [lax.dynamic_slice_in_dim(w_qkv, n * D + z * HEAD, HEAD, 1) for n in range(3)]

    pieces = relay(payload)
    others = [flip(piece, "core", 1, 2) for piece in pieces]
    do = lax.all_to_all(parts, ("z", "core"), 0, 0, tiled=True)
    normed, mine, part = head_pass(meta, pieces, others, do, gain, w_head)
    came = flip(part, "core", 1, 2)
    here, there = weight_pass(meta, normed, part, came)
    back = join_pass(meta, part, came)
    back = lax.all_to_all(back, "z", 0, 0, tiled=True)

    here = turn(here)
    there = turn(there, 0, 1)
    w_sum = added(here, there)
    w_sum = added(w_sum, flip(w_sum, "x", 1, 4))
    w_sum = added(w_sum, flip(w_sum, "x", 2, 4))
    w_sum = added(w_sum, flip(w_sum, "y_hi", 1, 2))
    w_sum = lax.all_to_all(w_sum, "z", 0, 0, tiled=True)
    other = flip(w_sum, "core", 1, 2)
    w_grad = final_pass(meta, w_sum, other)

    d_rows = rows_pass(back, mine, gain, w_qkv)
    d_rows = turn(d_rows)
    return (d_rows[None], w_grad)


def solution(mesh):
    fine = Mesh(
        mesh.devices.reshape(2, 8, 4, 2, 2), ("y_lo", "z", "x", "y_hi", "core")
    )
    seq = ("y_lo", "z")
    dp = ("x", "y_hi", "core")
    return jax.shard_map(
        work,
        mesh=fine,
        in_specs=(
            P(dp, seq, None),
            P(dp, seq),
            P(dp, None),
            P(),
            P(),
            P(dp, seq, None),
        ),
        out_specs=(P(dp, seq, None), P(seq, None)),
        check_vma=False,
    )
```
